32 devices in a mesh: rep: 4 (over x, core), exp: 8 (over z, y).
Axes of the slice: x: 2, y: 2, z: 4, core: 2. Of those that a mesh axis runs over, the one named last changes fastest.
Arguments:
- inputs: bfloat16 [4096, 2048], P(('rep', 'exp')), may hold values from -6 to 6
- out_grad: bfloat16 [4096, 2048], P(('rep', 'exp')), may hold values from -6 to 6
- routes: int32 [4096, 8], P(('rep', 'exp')), may hold values from 0 to 63, all different within a row; in each aligned block of 128 rows (0 to 127, 128 to 255, ...) at most 18 rows name the same one
- gates: float32 [4096, 8], P(('rep', 'exp')), may hold values from 0.05 to 0.3
- weights: bfloat16 [2048, 64, 3, 384], P('rep', 'exp'), may hold values from -0.125 to 0.125
- moment_one: float32 [2048, 64, 3, 384], P('rep', 'exp'), may hold values from -18 to 18
- moment_two: float32 [2048, 64, 3, 384], P('rep', 'exp'), may hold values from 1 to 100
Outputs:
- input_grad: bfloat16 [4096, 2048], P(('rep', 'exp'))
- first_moment: float32 [2048, 64, 3, 384], P('rep', 'exp')
- second_moment: float32 [2048, 64, 3, 384], P('rep', 'exp')
- new_weights: bfloat16 [2048, 64, 3, 384], P('rep', 'exp')
The draws below stay inside these ranges and needn't reach their ends.
Inputs may be any that keep to these rules, and one draw needn't show every extreme that they name: `routes`: each row names 8 different experts. In the rows of one device no expert is named by more than 18 rows, a bound that some block reaches.
All inputs are finite; a program needn't handle non-finite values.
Results may differ from the reference program's by a relative error of at most 0.0064.
Values may be sent and summed in bfloat16 or wider, within the bound.
A program may use at most 384 MiB of HBM per device.

```python
import math
import jax
import jax.numpy as jnp
import numpy as np
from jax import lax

D = 2048
E = 64
FFN = 384
TOP = 8
TOK_DEV = 128
CAP = 18
TOKENS = 4096
N_REP = 4
N_EXP = 8


def shard_levels(stream_key, dims, shards, smallest, largest):
    gain = 1.0
    for dim, shards_of in shards:
        steps = jax.random.uniform(jax.random.fold_in(jax.random.fold_in(stream_key, 6), dim), (shards_of,), jnp.float32, smallest / len(shards), largest / len(shards))
        gain = gain * jnp.repeat(jnp.exp(steps), dims[dim] // shards_of).reshape((-1,) + (1,) * (len(dims) - 1 - dim))
    return gain


def deal_out(own_key, own, number, rows, number_of, top, bound, slope):
    ranking = jax.random.permutation(own_key, number_of)
    crowded, ordinary = shares(number_of, rows * top, bound, slope, True), shares(number_of, rows * top, bound, slope, False)
    places = jnp.arange(number_of)

    def named(lengths, turn):
        used = int((lengths > 0).sum())
        fixed = max(1, used // 4)
        shifted = fixed + (places - fixed + turn * (used - fixed)) % max(1, number_of - fixed)
        return jnp.zeros((number_of,), jnp.int32).at[ranking[jnp.where(places < fixed, places, shifted)]].set(jnp.asarray(lengths, jnp.int32))

    lengths = jnp.where(number % 4 == 0, named(crowded, number // 4), named(ordinary, number - number // 4 - 1))
    mixed = jax.random.permutation(jax.random.fold_in(own, 3), number_of)
    source_of, receiver = mixed[0:number_of // 2 * 2:2], mixed[1:number_of // 2 * 2:2]
    room = jnp.minimum(lengths[source_of] - 1, bound - lengths[receiver]) // 2
    room = jnp.where((source_of == ranking[0]) | (receiver == ranking[0]) | (lengths[receiver] == 0), 0, jnp.maximum(room, 0))
    shifted = jax.random.randint(jax.random.fold_in(own, 4), (number_of // 2,), 0, 1 << 20) % (room + 1)
    lengths = lengths.at[source_of].add(-shifted).at[receiver].add(shifted)
    members = jnp.searchsorted(jnp.cumsum(lengths), jnp.arange(rows * top), side="right").astype(jnp.int32)
    grid = members.reshape(top, rows).T
    grid = grid[jax.random.permutation(jax.random.fold_in(own, 1), rows)]
    turn = jax.random.randint(jax.random.fold_in(own, 2), (rows, 1), 0, top)
    return jnp.take_along_axis(grid, (jnp.arange(top)[None, :] + turn) % top, axis=1)


def shares(number_of, total, most, skew, full):
    loads = [(1 << 20) // math.isqrt(grade ** skew) + 1 for grade in range(1, number_of + 1)]
    largest = most if full else min(most, max(-(-total // number_of), total * loads[0] // sum(loads)))
    least = 1 if total - largest >= number_of - 1 else 0
    given, rest = [largest] + [least] * (number_of - 1), total - largest - least * (number_of - 1)
    while rest > 0:
        movable = [i for i in range(1, number_of) if given[i] < largest] or [i for i in range(1, number_of) if given[i] < most]
        pool, left = sum([loads[i] for i in movable]), rest
        for i in movable:
            addition = min(most - given[i], max(1, left * loads[i] // pool), rest)
            given[i] = given[i] + addition
            rest = rest - addition
    return np.array(given)


def bell_draw(rng, dims, width, most, pieces=(), kind=jnp.bfloat16):
    values = width * jax.random.normal(rng, dims, jnp.float32)
    if pieces:
        values = values * shard_levels(rng, dims, pieces, -0.22, 0.18)
    return jnp.clip(values, -most, most).astype(kind)


def setup_inputs(seed: int = 0) -> dict:
    arg_keys = jax.random.split(jax.random.key(seed), 8)
    inputs = bell_draw(arg_keys[0], (TOKENS, D), 1.0, 6.0, ((0, 32),))
    out_grad = bell_draw(arg_keys[1], (TOKENS, D), 1.0, 6.0, ((0, 32),))
    routes_keys = jax.random.split(jax.random.fold_in(arg_keys[2], 1), TOKENS // TOK_DEV)
    routes_turns = jax.random.permutation(jax.random.fold_in(arg_keys[2], 3), TOKENS // TOK_DEV)
    routes = jax.vmap(lambda own, number: deal_out(jax.random.fold_in(arg_keys[2], 2), own, number, TOK_DEV, E, TOP, CAP, 0))(routes_keys, routes_turns).reshape((TOKENS, TOP))
    gates = jnp.clip(0.05 + 0.25 * jax.random.uniform(arg_keys[3], (TOKENS, TOP), jnp.float32) ** shard_levels(arg_keys[3], (TOKENS, TOP), ((0, 32),), -0.2, 0.2), 0.05, 0.3)
    weights = bell_draw(arg_keys[4], (D, E, 3, FFN), D ** -0.5, 0.125, ((0, 4), (1, 8)))
    moment_one = bell_draw(arg_keys[5], (D, E, 3, FFN), 3.0, 18.0, ((0, 4), (1, 8)), jnp.float32)
    moment_two = jnp.clip(jnp.exp(math.log(100.0) - 4.6051702 * jax.random.uniform(arg_keys[6], (D, E, 3, FFN), jnp.float32) ** shard_levels(arg_keys[6], (D, E, 3, FFN), ((0, 4), (1, 8)), -0.2, 0.2)), 1.0, 100.0)
    return {"inputs": inputs, "out_grad": out_grad, "routes": routes, "gates": gates, "weights": weights, "moment_one": moment_one, "moment_two": moment_two}


beta_one = 0.9
beta_two = 0.95
learn_rate = 0.002
decay_rate = 0.1
epsilon = 1e-08
step_count = 100

def slot_positions(routes):
    blocks = routes.reshape(N_REP * N_EXP, TOK_DEV * TOP)
    expert_ids = jnp.arange(E, dtype=jnp.int32)

    def one_block(block):
        onehot = (block[:, None] == expert_ids[None, :]).astype(jnp.int32)
        before = jnp.cumsum(onehot, axis=0) - onehot
        slot = lax.optimization_barrier(jnp.sum(before * onehot, axis=1))
        return block * CAP + slot
    return jax.vmap(one_block)(blocks)

def reference(inputs, out_grad, routes, gates, weights, moment_one, moment_two):
    nblocks = N_REP * N_EXP
    position = slot_positions(routes)
    pair_ids = jnp.broadcast_to(jnp.arange(TOK_DEV * TOP, dtype=jnp.int32)[None, :], position.shape)
    block_ids = jnp.broadcast_to(jnp.arange(nblocks, dtype=jnp.int32)[:, None], position.shape)
    table = jnp.full((nblocks, E * CAP), -1, jnp.int32).at[block_ids, position].set(pair_ids)

    def per_expert(carry, expert):
        cols = lax.dynamic_slice_in_dim(table, (expert * CAP).astype(jnp.int32), CAP, 1)
        valid = cols >= 0
        safe = jnp.where(valid, cols, 0)
        token = (jnp.arange(nblocks, dtype=jnp.int32)[:, None] * TOK_DEV + safe // TOP).astype(jnp.int32)
        pair_k = (safe % TOP).astype(jnp.int32)
        rows_x = jnp.where(valid[..., None], inputs[token], jnp.zeros((), inputs.dtype)).reshape(-1, D)
        gate = gates[token, pair_k]
        scaled = (gate[..., None] * out_grad[token].astype(jnp.float32)).astype(jnp.bfloat16)
        rows_g = jnp.where(valid[..., None], scaled, jnp.zeros((), scaled.dtype)).reshape(-1, D)
        mats = weights[:, expert]
        w_gate = mats[:, 0]
        w_up = mats[:, 1]
        w_down = mats[:, 2]
        hg = jnp.dot(rows_x, w_gate, preferred_element_type=jnp.float32)
        hu = jnp.dot(rows_x, w_up, preferred_element_type=jnp.float32)
        sig = jax.nn.sigmoid(hg)
        act = (hg * sig * hu).astype(jnp.bfloat16)
        da = jnp.dot(rows_g, w_down, preferred_element_type=jnp.float32)
        dhu = (da * hg * sig).astype(jnp.bfloat16)
        dhg = (da * hu * sig * (1.0 + hg * (1.0 - sig))).astype(jnp.bfloat16)
        slot_dx = (jnp.dot(dhg, w_gate.T, preferred_element_type=jnp.float32) + jnp.dot(dhu, w_up.T, preferred_element_type=jnp.float32)).astype(jnp.bfloat16)
        g_gate = jnp.dot(rows_x.T, dhg, preferred_element_type=jnp.float32)
        g_up = jnp.dot(rows_x.T, dhu, preferred_element_type=jnp.float32)
        g_down = jnp.dot(rows_g.T, act, preferred_element_type=jnp.float32)
        carry = carry.at[token.reshape(-1)].add(slot_dx.astype(jnp.float32))
        return (carry, jnp.stack([g_gate, g_up, g_down], axis=1))
    start = jnp.zeros((N_REP * N_EXP * TOK_DEV, D), jnp.float32)
    dx_total, grads = lax.scan(per_expert, start, jnp.arange(E, dtype=jnp.int32))
    grad = jnp.transpose(grads, (1, 0, 2, 3))
    first_moment = beta_one * moment_one + (1.0 - beta_one) * grad
    second_moment = beta_two * moment_two + (1.0 - beta_two) * grad * grad
    correct_one = 1.0 - beta_one ** step_count
    correct_two = 1.0 - beta_two ** step_count
    weights32 = weights.astype(jnp.float32)
    update = first_moment / correct_one / (jnp.sqrt(second_moment / correct_two) + epsilon) + decay_rate * weights32
    new_weights = (weights32 - learn_rate * update).astype(jnp.bfloat16)
    return (dx_total.astype(jnp.bfloat16), first_moment, second_moment, new_weights)
```

```python
import functools

import jax
import jax.numpy as jnp
from jax import lax
from jax.experimental import pallas as pl
from jax.experimental.pallas import tpu as pltpu
from jax.sharding import PartitionSpec as P


CAP = 18


beta_one = 0.9
beta_two = 0.95
learn_rate = 0.002
decay_rate = 0.1
epsilon = 1e-08
step_count = 100

F32 = jnp.float32
BF16 = jnp.bfloat16


def update_kernel(dims, *refs):
    (replicas, slots, part, local, kinds, ffn, block, depth, _) = dims
    pieces, refs = refs[: 4 * replicas], refs[4 * replicas :]
    m_one, m_two, w_in, o_one, o_two, w_out = refs[:6]
    bufs, (grad, b_one, b_two, b_w, in_sem, load_sem, store_sem) = refs[6:10], refs[10:]
    rows = replicas * slots
    twin = min(2, local)
    blocks = part // block
    ahead = min(depth, blocks)
    lanes = grad.shape[2]

    def fetch(e, go):
        for kind in range(4):
            for q in range(replicas):
                n = kind * replicas + q
                copy = pltpu.make_async_copy(
                    pieces[n].at[e],
                    bufs[kind].at[lax.rem(e, twin), pl.ds(q * slots, slots)],
                    in_sem.at[lax.rem(e, twin), n],
                )
                copy.start() if go else copy.wait()

    def moves(i, outward):
        s = lax.rem(i, depth)
        part_of = pl.ds(i * block, block)
        if outward:
            trio = ((b_one, o_one), (b_two, o_two), (b_w, w_out))
            return [
                pltpu.make_async_copy(a.at[s], b.at[part_of], store_sem.at[n, s])
                for n, (a, b) in enumerate(trio)
            ]
        trio = ((b_one, m_one), (b_two, m_two), (b_w, w_in))
        return [
            pltpu.make_async_copy(b.at[part_of], a.at[s], load_sem.at[n, s])
            for n, (a, b) in enumerate(trio)
        ]

    fetch(0, True)

    @pl.loop(0, ahead)
    def _(i):
        for copy in moves(i, False):
            copy.start()

    @pl.loop(0, local)
    def _(e):
        if twin > 1:

            @pl.when(e + 1 < local)
            def _():
                fetch(e + 1, True)

        fetch(e, False)
        at = lax.rem(e, twin)
        base = pl.multiple_of(e * part, part)
        step = rows if rows <= 1024 else slots
        for lead, width, left, right in ((0, 2 * ffn, 0, 2), (2 * ffn, ffn, 1, 3)):
            for start in range(0, rows, step):
                one = lax.dot_general(
                    bufs[left][at, pl.ds(start, step), :],
                    bufs[right][at, pl.ds(start, step), :],
                    (((0,), (0,)), ((), ())),
                    preferred_element_type=F32,
                )
                for c in range(width // lanes):
                    tile = one[:, c * lanes : (c + 1) * lanes]
                    place = lead // lanes + c
                    if start:
                        tile = tile + grad[place, pl.ds(base, part), :]
                    grad[place, pl.ds(base, part), :] = tile

    correct_one = 1.0 - beta_one**step_count
    correct_two = 1.0 - beta_two**step_count

    @pl.loop(0, blocks)
    def _(i):
        s = lax.rem(i, depth)
        for copy in moves(i, False):
            copy.wait()

        @pl.loop(0, block // 4)
        def _(pair):
            spots = []
            for sub in range(4):
                row = pair * 4 + sub
                d = i * block + row
                of_d = pl.ds(d, local, stride=part) if local > 1 else pl.ds(d, 1)
                for place in range(kinds * ffn // lanes):
                    kind, c = divmod(place * lanes, ffn)
                    spots.append(((s, row, kind, slice(None), pl.ds(c, lanes)), place, of_d))
            held = [(b_one[at], b_two[at], b_w[at], grad[place, of_d, :]) for at, place, of_d in spots]
            done = []
            for one, two, w, g in held:
                first = beta_one * one + (1.0 - beta_one) * g
                second = beta_two * two + (1.0 - beta_two) * g * g
                w = w.astype(F32)
                root = jnp.sqrt(second * (1.0 / correct_two)) + epsilon
                update = first * (1.0 / correct_one) / root + decay_rate * w
                done.append((first, second, (w - learn_rate * update).astype(BF16)))
            for (at, _, _), (first, second, new) in zip(spots, done):
                b_one[at] = first
                b_two[at] = second
                b_w[at] = new

        for copy in moves(i, True):
            copy.start()

        @pl.when((i >= 1) & (i - 1 + depth < blocks))
        def _():
            for copy in moves(i - 1, True):
                copy.wait()
            for copy in moves(i - 1 + depth, False):
                copy.start()

    @pl.loop(max(blocks - depth, 0), blocks)
    def _(i):
        for copy in moves(i, True):
            copy.wait()


def expert_update(rows_x, rows_g, d_pair, acts, weights, moment_one, moment_two):
    replicas = len(rows_x)
    local, slots, part = rows_x[0].shape
    kinds, ffn = weights.shape[2:]
    block = 32
    twin = min(2, local)
    rows = replicas * slots
    pieces = [a[q] for a in (rows_x, rows_g, d_pair, acts) for q in range(replicas)]
    held = [a.transpose(0, 2, 1, 3) for a in (moment_one, moment_two, weights)]
    depth = 10
    any_spec = pl.BlockSpec(memory_space=pl.ANY)
    kernel = functools.partial(
        update_kernel, (replicas, slots, part, local, kinds, ffn, block, depth, None)
    )
    outs = pl.pallas_call(
        kernel,
        out_shape=tuple(jax.ShapeDtypeStruct(a.shape, a.dtype) for a in held),
        in_specs=[any_spec] * (len(pieces) + 3),
        out_specs=(any_spec,) * 3,
        scratch_shapes=[
            pltpu.VMEM((twin, rows, part), BF16),
            pltpu.VMEM((twin, rows, part), BF16),
            pltpu.VMEM((twin, rows, 2 * ffn), BF16),
            pltpu.VMEM((twin, rows, ffn), BF16),
            pltpu.VMEM((kinds * ffn // 128, local * part, 128), F32),
            pltpu.VMEM((depth, block, kinds, local, ffn), F32),
            pltpu.VMEM((depth, block, kinds, local, ffn), F32),
            pltpu.VMEM((depth, block, kinds, local, ffn), BF16),
            pltpu.SemaphoreType.DMA((twin, 4 * replicas)),
            pltpu.SemaphoreType.DMA((3, depth)),
            pltpu.SemaphoreType.DMA((3, depth)),
        ],
        compiler_params=pltpu.CompilerParams(vmem_limit_bytes=60 << 20),
        cost_estimate=pl.CostEstimate(
            flops=2 * rows * part * kinds * ffn * local,
            bytes_accessed=2 * sum(a.size * a.dtype.itemsize for a in held),
            transcendentals=0,
        ),
        name="expert_update",
    )(*pieces, *held)
    return [a.transpose(0, 2, 1, 3) for a in outs]


def per_device(inputs, out_grad, routes, gates, weights, moment_one, moment_two):
    replicas, sources = lax.axis_size("rep"), lax.axis_size("exp")
    tok_dev, top = routes.shape
    part, local, kinds, ffn = weights.shape
    pair = 2 * ffn
    slots = sources * CAP
    me = lax.axis_index("rep")

    def swap(array, bits):
        if bits == 0:
            return array
        return lax.ppermute(array, "rep", [(i, i ^ bits) for i in range(replicas)])

    terms, rest = [routes.astype(BF16).T], gates.T
    for _ in range(3):
        head = lax.reduce_precision(rest, 8, 7)
        terms.append(head.astype(BF16))
        rest = rest - head
    meta = jnp.concatenate(terms).reshape(-1, part)
    meta_rows = meta.shape[0]
    pad = -meta_rows % 16
    meta = jnp.pad(meta, ((0, pad), (0, 0)))

    def arrive(q):
        at = (me ^ q) * part
        x = lax.dynamic_slice_in_dim(inputs, at, part, 1)
        g = lax.dynamic_slice_in_dim(out_grad, at, part, 1)
        return swap(jnp.concatenate([x, g, meta]), q)

    gathered = {}
    half = max(replicas // 2, 1)
    for start in range(replicas - half, -1, -half):
        chosen = range(start, start + half)
        block = jnp.stack([arrive(q) for q in reversed(chosen)])
        block = lax.all_gather(block, "exp", axis=0, tiled=False)
        for place, q in enumerate(reversed(chosen)):
            gathered[q] = block[:, place]

    mine = lax.axis_index("exp") * local + jnp.arange(local, dtype=jnp.int32)
    earlier = jnp.arange(tok_dev)[:, None] < jnp.arange(tok_dev)[None, :]
    base = (jnp.arange(sources) * CAP).astype(F32)
    mats = weights.transpose(1, 0, 2, 3).reshape(local, part, kinds * ffn)
    pair_mats, down_mats = mats[..., :pair], mats[..., pair:]
    picks, rows_x, rows_g, arrivals = {}, {}, {}, {}
    for q in reversed(range(replicas)):
        if q == half - 1 and replicas > 1:
            later = {p: gathered[p] for p in range(half)}
            later, _ = lax.optimization_barrier((later, sent))
            gathered.update(later)
        got = gathered[q]
        info = got[:, 2 * tok_dev : 2 * tok_dev + meta_rows].astype(F32)
        info = info.reshape(sources, 4, top, tok_dev)
        weight = info[:, 1] + info[:, 2] + info[:, 3]
        hit = info[:, 0][None] == mine.astype(F32)[:, None, None, None]
        named = jnp.any(hit, axis=2)
        gate = jnp.sum(jnp.where(hit, weight[None], 0.0), axis=2)
        rank = jnp.einsum(
            "let,tu->leu", named.astype(BF16), earlier.astype(BF16), preferred_element_type=F32
        )
        rank = jnp.where(named, rank + base[None, :, None], -1.0)
        rank = rank.reshape(local, 1, sources * tok_dev)
        onehot = rank == jnp.arange(slots, dtype=F32)[None, :, None]
        gate = gate.reshape(local, 1, sources * tok_dev)
        gate_slot = jnp.sum(jnp.where(onehot, gate, 0.0), axis=2)
        picks[q] = onehot.astype(BF16)
        tokens_x = got[:, :tok_dev].reshape(sources * tok_dev, part)
        tokens_g = got[:, tok_dev : 2 * tok_dev].reshape(sources * tok_dev, part)
        x = jnp.einsum("lst,td->lsd", picks[q], tokens_x, preferred_element_type=F32)
        g = jnp.einsum("lst,td->lsd", picks[q], tokens_g, preferred_element_type=F32)
        rows_x[q] = x.astype(BF16)
        rows_g[q] = (g * gate_slot[..., None]).astype(BF16)
        hidden = jnp.einsum("lrd,ldh->lrh", rows_x[q], pair_mats, preferred_element_type=F32)
        da = jnp.einsum("lrd,ldh->lrh", rows_g[q], down_mats, preferred_element_type=F32)
        sums = [hidden, da]
        for term in arrivals.pop(q, []):
            sums = [old + new.astype(F32) for old, new in zip(sums, term)]
        sent = [one.astype(BF16) for one in sums]
        if q:
            arrivals.setdefault(q & (q - 1), []).append([swap(one, q & -q) for one in sent])

    hidden, da = sums
    hg, hu = hidden[..., :ffn], hidden[..., ffn:]
    sig = jax.nn.sigmoid(hg)
    act = (hg * sig * hu).astype(BF16)
    dhu = (da * hg * sig).astype(BF16)
    dhg = (da * hu * sig * (1.0 + hg * (1.0 - sig))).astype(BF16)
    d_pair, acts = {0: jnp.concatenate([dhg, dhu], axis=2)}, {0: act}
    for held in (d_pair, acts):
        bit = replicas // 2
        while bit:
            for q in list(held):
                held[q ^ bit] = swap(held[q], bit)
            bit //= 2

    token_dx = {}
    for q in range(replicas):
        slot_dx = jnp.einsum(
            "lrh,ldh->lrd", d_pair[q], pair_mats, preferred_element_type=F32
        ).astype(BF16)
        dx = jnp.einsum("lst,lsd->td", picks[q], slot_dx, preferred_element_type=F32)
        token_dx[q] = dx.astype(BF16).reshape(sources, tok_dev, part)
    home = {}
    for start in range(0, replicas, half):
        block = jnp.concatenate([token_dx[q] for q in range(start, start + half)], axis=1)
        block = lax.psum_scatter(block, "exp", scatter_dimension=0, tiled=False)
        for place in range(half):
            one = block[place * tok_dev : (place + 1) * tok_dev]
            home[start + place] = swap(one, start + place)
    home = jnp.stack([home[q] for q in range(replicas)])
    input_grad = jnp.concatenate(
        [lax.dynamic_index_in_dim(home, me ^ q, 0, keepdims=False) for q in range(replicas)],
        axis=1,
    )

    first_moment, second_moment, new_weights = expert_update(
        rows_x, rows_g, d_pair, acts, weights, moment_one, moment_two
    )
    return (input_grad, first_moment, second_moment, new_weights)


def solution(mesh):
    tokens = P(("rep", "exp"), None)
    experts = P("rep", "exp", None, None)
    return jax.shard_map(
        per_device,
        mesh=mesh,
        in_specs=(tokens, tokens, tokens, tokens, experts, experts, experts),
        out_specs=(tokens, experts, experts, experts),
        check_vma=False,
    )
```

```python
import functools

import jax
import jax.numpy as jnp
from jax import lax
from jax.experimental import pallas as pl
from jax.experimental.pallas import tpu as pltpu
from jax.sharding import PartitionSpec as P


CAP = 18


beta_one = 0.9
beta_two = 0.95
learn_rate = 0.002
decay_rate = 0.1
epsilon = 1e-08
step_count = 100

F32 = jnp.float32
BF16 = jnp.bfloat16


def update_kernel(dims, *refs):
    (replicas, slots, part, local, kinds, ffn, block, depth, _) = dims
    pieces, refs = refs[:4], refs[4:]
    m_one, m_two, w_in, o_one, o_two, w_out = refs[:6]
    bufs, (grad, b_one, b_two, b_w, in_sem, load_sem, store_sem) = refs[6:10], refs[10:]
    rows = replicas * slots
    twin = min(2, local)
    blocks = part // block
    ahead = min(depth, blocks)
    lanes = grad.shape[2]

    def fetch(e, go):
        for kind in range(4):
            for q in range(replicas):
                n = kind * replicas + q
                copy = pltpu.make_async_copy(
                    pieces[kind].at[q, e],
                    bufs[kind].at[lax.rem(e, twin), pl.ds(q * slots, slots)],
                    in_sem.at[lax.rem(e, twin), n],
                )
                copy.start() if go else copy.wait()

    def moves(i, outward):
        s = lax.rem(i, depth)
        part_of = pl.ds(i * block, block)
        if outward:
            trio = ((b_one, o_one), (b_two, o_two), (b_w, w_out))
            return [
                pltpu.make_async_copy(a.at[s], b.at[part_of], store_sem.at[n, s])
                for n, (a, b) in enumerate(trio)
            ]
        trio = ((b_one, m_one), (b_two, m_two), (b_w, w_in))
        return [
            pltpu.make_async_copy(b.at[part_of], a.at[s], load_sem.at[n, s])
            for n, (a, b) in enumerate(trio)
        ]

    fetch(0, True)

    @pl.loop(0, ahead)
    def _(i):
        for copy in moves(i, False):
            copy.start()

    @pl.loop(0, local)
    def _(e):
        if twin > 1:

            @pl.when(e + 1 < local)
            def _():
                fetch(e + 1, True)

        fetch(e, False)
        at = lax.rem(e, twin)
        base = pl.multiple_of(e * part, part)
        step = rows if rows <= 1024 else slots
        for lead, width, left, right in ((0, 2 * ffn, 0, 2), (2 * ffn, ffn, 1, 3)):
            for start in range(0, rows, step):
                one = lax.dot_general(
                    bufs[left][at, pl.ds(start, step), :],
                    bufs[right][at, pl.ds(start, step), :],
                    (((0,), (0,)), ((), ())),
                    preferred_element_type=F32,
                )
                for c in range(width // lanes):
                    tile = one[:, c * lanes : (c + 1) * lanes]
                    place = lead // lanes + c
                    if start:
                        tile = tile + grad[place, pl.ds(base, part), :]
                    grad[place, pl.ds(base, part), :] = tile

    correct_one = 1.0 - beta_one**step_count
    correct_two = 1.0 - beta_two**step_count

    @pl.loop(0, blocks)
    def _(i):
        s = lax.rem(i, depth)
        for copy in moves(i, False):
            copy.wait()

        @pl.loop(0, block // 4)
        def _(pair):
            spots = []
            for sub in range(4):
                row = pair * 4 + sub
                d = i * block + row
                of_d = pl.ds(d, local, stride=part) if local > 1 else pl.ds(d, 1)
                for place in range(kinds * ffn // lanes):
                    kind, c = divmod(place * lanes, ffn)
                    spots.append(((s, row, kind, slice(None), pl.ds(c, lanes)), place, of_d))
            held = [(b_one[at], b_two[at], b_w[at], grad[place, of_d, :]) for at, place, of_d in spots]
            done = []
            for one, two, w, g in held:
                first = beta_one * one + (1.0 - beta_one) * g
                second = beta_two * two + (1.0 - beta_two) * g * g
                w = w.astype(F32)
                root = jnp.sqrt(second * (1.0 / correct_two)) + epsilon
                update = first * (1.0 / correct_one) / root + decay_rate * w
                done.append((first, second, (w - learn_rate * update).astype(BF16)))
            for (at, _, _), (first, second, new) in zip(spots, done):
                b_one[at] = first
                b_two[at] = second
                b_w[at] = new

        for copy in moves(i, True):
            copy.start()

        @pl.when((i >= 1) & (i - 1 + depth < blocks))
        def _():
            for copy in moves(i - 1, True):
                copy.wait()
            for copy in moves(i - 1 + depth, False):
                copy.start()

    @pl.loop(max(blocks - depth, 0), blocks)
    def _(i):
        for copy in moves(i, True):
            copy.wait()


def expert_update(rows_x, rows_g, d_pair, acts, weights, moment_one, moment_two):
    replicas, local, slots, part = rows_x.shape
    kinds, ffn = weights.shape[2:]
    block = 32
    twin = min(2, local)
    rows = replicas * slots
    pieces = (rows_x, rows_g, d_pair, acts)
    held = [a.transpose(0, 2, 1, 3) for a in (moment_one, moment_two, weights)]
    depth = 10
    any_spec = pl.BlockSpec(memory_space=pl.ANY)
    kernel = functools.partial(
        update_kernel, (replicas, slots, part, local, kinds, ffn, block, depth, None)
    )
    outs = pl.pallas_call(
        kernel,
        out_shape=tuple(jax.ShapeDtypeStruct(a.shape, a.dtype) for a in held),
        in_specs=[any_spec] * (len(pieces) + 3),
        out_specs=(any_spec,) * 3,
        scratch_shapes=[
            pltpu.VMEM((twin, rows, part), BF16),
            pltpu.VMEM((twin, rows, part), BF16),
            pltpu.VMEM((twin, rows, 2 * ffn), BF16),
            pltpu.VMEM((twin, rows, ffn), BF16),
            pltpu.VMEM((kinds * ffn // 128, local * part, 128), F32),
            pltpu.VMEM((depth, block, kinds, local, ffn), F32),
            pltpu.VMEM((depth, block, kinds, local, ffn), F32),
            pltpu.VMEM((depth, block, kinds, local, ffn), BF16),
            pltpu.SemaphoreType.DMA((twin, 4 * replicas)),
            pltpu.SemaphoreType.DMA((3, depth)),
            pltpu.SemaphoreType.DMA((3, depth)),
        ],
        compiler_params=pltpu.CompilerParams(vmem_limit_bytes=60 << 20),
        cost_estimate=pl.CostEstimate(
            flops=2 * rows * part * kinds * ffn * local,
            bytes_accessed=2 * sum(a.size * a.dtype.itemsize for a in held),
            transcendentals=0,
        ),
        name="expert_update",
    )(*pieces, *held)
    return [a.transpose(0, 2, 1, 3) for a in outs]


MESH = pl.DeviceIdType.MESH


def flip(index, bits):
    for bit in (1, 2):
        if bits & bit:
            index = index + bit * (1 - 2 * ((index // bit) % 2))
    return index


def forward_kernel(dims, x, g, meta, weights, out_x, out_g, out_pair, out_act, out_rank, *scratch):
    replicas, sources, tok, part, local, slots, ffn, cap = dims
    (gx, gg, gm, w, rank, gate, rows_x, rows_g, outgoing, incoming, own, held, raw, turned) = scratch[:14]
    (own_send, got, sent, w_sem, part_send, part_got, d_send, d_got, out_sem) = scratch[14:]
    me, ex = lax.axis_index("rep"), lax.axis_index("exp")
    col, z = ex % 2, ex // 2
    line = sources // 2
    side = ex + 1 - 2 * col
    above, below = z + 1 < line, z >= 1
    pair = 2 * ffn
    order = tuple(reversed(range(replicas)))
    kinds = ((gm, meta), (gx, x), (gg, g))

    barrier = pltpu.get_barrier_semaphore()
    for q in order[:-1]:
        pl.semaphore_signal(barrier, inc=1, device_id={"rep": flip(me, q)}, device_id_type=MESH)
    pl.semaphore_signal(barrier, inc=1, device_id={"exp": side}, device_id_type=MESH)

    @pl.when(above)
    def _():
        pl.semaphore_signal(barrier, inc=1, device_id={"exp": ex + 2}, device_id_type=MESH)

    @pl.when(below)
    def _():
        pl.semaphore_signal(barrier, inc=1, device_id={"exp": ex - 2}, device_id_type=MESH)

    lanes = turned.shape[2]
    chunk = raw.shape[1]
    chunks = part // chunk

    def load_w(c):
        return pltpu.make_async_copy(
            weights.at[pl.ds(c * chunk, chunk)], raw.at[c % 2], w_sem.at[c % 2]
        )

    def turn(c):
        if c + 1 < chunks:
            load_w(c + 1).start()
        load_w(c).wait()
        unroll = 4

        @pl.loop(0, chunk // unroll)
        def _(d4):
            for sub in range(unroll):
                d = d4 * unroll + sub
                for place in range(3 * ffn // lanes):
                    kind, at = divmod(place * lanes, ffn)
                    tile = raw[c % 2, d, kind, :, pl.ds(at, lanes)].astype(F32)
                    turned[place, pl.ds(d, local, stride=chunk), :] = tile

        @pl.loop(0, local)
        def _(l):
            for place in range(3 * ffn // lanes):
                tile = turned[place, pl.ds(pl.multiple_of(l * chunk, chunk), chunk), :]
                w[l, pl.ds(c * chunk, chunk), pl.ds(place * lanes, lanes)] = tile.astype(BF16)

    load_w(0).start()
    expected = replicas + jnp.where(above, 1, 0) + jnp.where(below, 1, 0)
    pl.semaphore_wait(barrier, expected)

    def first(q, n):
        buf, src = kinds[n]
        target = flip(me, q)
        if n:
            src = src.at[:, pl.ds(pl.multiple_of(target * part, part), part)]
        if q == 0:
            return pltpu.make_async_copy(src, buf.at[q, ex], got.at[q, n, ex])
        return pltpu.make_async_remote_copy(
            src_ref=src,
            dst_ref=buf.at[q, ex],
            send_sem=own_send.at[q, n],
            recv_sem=got.at[q, n, ex],
            device_id={"rep": target},
            device_id_type=MESH,
        )

    def hop(q, n, slot, way):
        target = (side, ex + 2, ex - 2)[way]
        return pltpu.make_async_remote_copy(
            src_ref=kinds[n][0].at[q, slot],
            dst_ref=kinds[n][0].at[q, slot],
            send_sem=sent.at[way, q, n, slot],
            recv_sem=got.at[q, n, slot],
            device_id={"exp": target},
            device_id_type=MESH,
        )

    for q in order:
        for n in range(3):
            first(q, n).start()

    def relay(q, step):
        for n in range(3):
            if step == 0:
                if q:
                    first(q, n).wait_recv()
                else:
                    first(q, n).wait()
                hop(q, n, ex, 0).start()

                @pl.when(above)
                def _():
                    hop(q, n, ex, 1).start()

                @pl.when(below)
                def _():
                    hop(q, n, ex, 2).start()

                continue

            @pl.when(z >= step)
            def _():
                slot = ex - 2 * step
                hop(q, n, slot, 0).wait_recv()
                hop(q, n, slot, 0).start()

                @pl.when(above)
                def _():
                    hop(q, n, slot, 1).start()

            @pl.when(z + step < line)
            def _():
                slot = ex + 2 * step
                hop(q, n, slot, 0).wait_recv()
                hop(q, n, slot, 0).start()

                @pl.when(below)
                def _():
                    hop(q, n, slot, 2).start()

    def settle(q):
        for n in range(3):
            for level in range(line):
                hop(q, n, 2 * level + 1 - col, 0).wait_recv()

    lower = lax.broadcasted_iota(jnp.int32, (tok, tok), 0)
    upper = lax.broadcasted_iota(jnp.int32, (tok, tok), 1)
    earlier = jnp.where(lower < upper, 1.0, 0.0).astype(BF16)
    expert0 = (ex * local).astype(F32)

    def prepare(q):
        @pl.loop(0, sources)
        def _(s):
            info = gm[q, s].astype(F32)[:8]
            routes = info[:, :tok]
            weight = info[:, tok : 2 * tok] + info[:, 2 * tok : 3 * tok] + info[:, 3 * tok :]
            named, gates = [], []
            for l in range(local):
                hit = routes == expert0 + l
                named.append(jnp.max(jnp.where(hit, 1.0, 0.0), axis=0, keepdims=True))
                gates.append(jnp.sum(jnp.where(hit, weight, 0.0), axis=0, keepdims=True))
            named = jnp.concatenate(named, axis=0)
            places = jnp.dot(named.astype(BF16), earlier, preferred_element_type=F32)
            places = jnp.where(named > 0.0, places + (s * cap).astype(F32), -1.0)
            at = pl.ds(pl.multiple_of(s * tok, tok), tok)
            rank[q, :, at] = places
            gate[:, at] = jnp.concatenate(gates, axis=0)

    def exchange(l, q):
        slot, into, bits = {3: (0, 0, 1), 2: (1, 2, 2), 1: (0, 1, 1)}[q]
        return pltpu.make_async_remote_copy(
            src_ref=outgoing.at[slot, l],
            dst_ref=incoming.at[into, l],
            send_sem=part_send.at[q, l],
            recv_sem=part_got.at[into, l],
            device_id={"rep": flip(me, bits)},
            device_id_type=MESH,
        )

    def row_out(l, q):
        return (
            pltpu.make_async_copy(rows_x.at[q, l], out_x.at[q, l], out_sem.at[0, q, l]),
            pltpu.make_async_copy(rows_g.at[q, l], out_g.at[q, l], out_sem.at[1, q, l]),
        )

    def piece(l, q):
        places = rank[q, pl.ds(l, 1), :]
        index = lax.broadcasted_iota(jnp.int32, (slots, sources * tok), 0).astype(F32)
        hit = index == places
        pick = jnp.where(hit, 1.0, 0.0).astype(BF16)
        gates = jnp.sum(jnp.where(hit, gate[pl.ds(l, 1), :], 0.0), axis=1, keepdims=True)
        tokens_x = gx[q].reshape(sources * tok, part)
        tokens_g = gg[q].reshape(sources * tok, part)
        rx = jnp.dot(pick, tokens_x, preferred_element_type=F32).astype(BF16)
        rg = (jnp.dot(pick, tokens_g, preferred_element_type=F32) * gates).astype(BF16)
        rows_x[q, l] = rx
        rows_g[q, l] = rg
        for copy in row_out(l, q):
            copy.start()
        hidden = jnp.dot(rx, w[l, :, :pair], preferred_element_type=F32)
        da = jnp.dot(rg, w[l, :, pair:], preferred_element_type=F32)
        for lead, width, one in ((0, pair, hidden), (pair, ffn, da)):
            at = pl.ds(lead, width)
            if q == 3:
                outgoing[0, l, :, at] = one.astype(BF16)
            elif q == 2:
                if not lead:
                    exchange(l, 3).wait_recv()
                outgoing[1, l, :, at] = (one + incoming[0, l, :, at].astype(F32)).astype(BF16)
            elif q == 1:
                if not lead:
                    exchange(l, 3).wait_send()
                outgoing[0, l, :, at] = one.astype(BF16)
            else:
                if not lead:
                    exchange(l, 1).wait_recv()
                own[l, :, at] = one + incoming[1, l, :, at].astype(F32)
        if q:
            exchange(l, q).start()

    def grads_to(l, way):
        src, dst, bits = ((0, 1, 1), (0, 2, 2), (2, 3, 1))[way]
        return pltpu.make_async_remote_copy(
            src_ref=held.at[src, l],
            dst_ref=held.at[dst, l],
            send_sem=d_send.at[way, l],
            recv_sem=d_got.at[way, l],
            device_id={"rep": flip(me, bits)},
            device_id_type=MESH,
        )

    def d_out(l, q):
        return (
            pltpu.make_async_copy(
                held.at[q, l, :, pl.ds(0, pair)], out_pair.at[q, l], out_sem.at[2, q, l]
            ),
            pltpu.make_async_copy(
                held.at[q, l, :, pl.ds(pair, ffn)], out_act.at[q, l], out_sem.at[3, q, l]
            ),
        )

    def finish(l):
        exchange(l, 2).wait_recv()
        sums = [
            own[l, :, pl.ds(n * ffn, ffn)] + incoming[2, l, :, pl.ds(n * ffn, ffn)].astype(F32)
            for n in range(3)
        ]
        hg, hu, da = sums
        sig = jax.nn.sigmoid(hg)
        held[0, l, :, pl.ds(2 * ffn, ffn)] = (hg * sig * hu).astype(BF16)
        held[0, l, :, pl.ds(ffn, ffn)] = (da * hg * sig).astype(BF16)
        held[0, l, :, pl.ds(0, ffn)] = (da * hu * sig * (1.0 + hg * (1.0 - sig))).astype(BF16)
        for way in (1, 0):
            grads_to(l, way).start()
        for copy in d_out(l, 0):
            copy.start()

    def pass_on(l):
        grads_to(l, 1).wait_recv()
        grads_to(l, 2).start()
        for copy in d_out(l, 2):
            copy.start()

    def pieces(lo, hi, q):
        @pl.loop(lo, hi)
        def _(l):
            piece(l, q)

    steps = max(line - 1, 1)
    turns = [range(chunks * n // (steps + 1), chunks * (n + 1) // (steps + 1)) for n in range(steps + 1)]
    for c in turns[0]:
        turn(c)
    relay(order[0], 0)
    for i, q in enumerate(order):
        if i + 1 < replicas:
            relay(order[i + 1], 0)
        for step in range(1, line):
            relay(q, step)
            if not i:
                for c in turns[step]:
                    turn(c)
            if i:
                pieces(local * (step - 1) // steps, local * step // steps, order[i - 1])
        settle(q)
        prepare(q)

    @pl.loop(0, local + 2)
    def _(l):
        @pl.when(l < local)
        def _():
            piece(l, order[-1])
            finish(l)

        @pl.when(l >= 2)
        def _():
            pass_on(l - 2)

    rank_copy = pltpu.make_async_copy(rank, out_rank, w_sem.at[0])
    rank_copy.start()

    @pl.loop(0, local)
    def _(l):
        grads_to(l, 0).wait_recv()
        for copy in d_out(l, 1):
            copy.start()
        grads_to(l, 2).wait_recv()
        for copy in d_out(l, 3):
            copy.start()

    rank_copy.wait()

    @pl.loop(0, local)
    def _(l):
        for q in (2, 1):
            exchange(l, q).wait_send()
        for way in range(3):
            grads_to(l, way).wait_send()
        for q in range(replicas):
            for copy in row_out(l, q) + d_out(l, q):
                copy.wait()

    for q in order:
        for n in range(3):
            if q:
                first(q, n).wait_send()

            @pl.loop(0, line)
            def _(level):
                slot = 2 * level + col
                hop(q, n, slot, 0).wait_send()

                @pl.when(above & (level <= z))
                def _():
                    hop(q, n, slot, 1).wait_send()

                @pl.when(below & (level >= z))
                def _():
                    hop(q, n, slot, 2).wait_send()


def forward(inputs, out_grad, meta, weights, replicas, sources, cap):
    tok = inputs.shape[0]
    part, local, kinds, ffn = weights.shape
    width = kinds * ffn
    chunk = part // 8
    slots = sources * cap
    dims = (replicas, sources, tok, part, local, slots, ffn, cap)
    any_spec = pl.BlockSpec(memory_space=pl.ANY)
    rows = (replicas, local, slots)
    dma = pltpu.SemaphoreType.DMA
    return pl.pallas_call(
        functools.partial(forward_kernel, dims),
        out_shape=(
            jax.ShapeDtypeStruct((*rows, part), BF16),
            jax.ShapeDtypeStruct((*rows, part), BF16),
            jax.ShapeDtypeStruct((*rows, 2 * ffn), BF16),
            jax.ShapeDtypeStruct((*rows, ffn), BF16),
            jax.ShapeDtypeStruct((replicas, local, sources * tok), F32),
        ),
        in_specs=[any_spec] * 4,
        out_specs=(any_spec,) * 5,
        scratch_shapes=[
            pltpu.VMEM((replicas, sources, tok, part), BF16),
            pltpu.VMEM((replicas, sources, tok, part), BF16),
            pltpu.VMEM((replicas, sources, *meta.shape), BF16),
            pltpu.VMEM((local, part, width), BF16),
            pltpu.VMEM((replicas, local, sources * tok), F32),
            pltpu.VMEM((local, sources * tok), F32),
            pltpu.VMEM((*rows, part), BF16),
            pltpu.VMEM((*rows, part), BF16),
            pltpu.VMEM((2, local, slots, width), BF16),
            pltpu.VMEM((3, local, slots, width), BF16),
            pltpu.VMEM((local, slots, width), F32),
            pltpu.VMEM((*rows, width), BF16),
            pltpu.VMEM((2, chunk, kinds, local, ffn), BF16),
            pltpu.VMEM((width // 128, local * chunk, 128), F32),
            dma((replicas, 3)),
            dma((replicas, 3, sources)),
            dma((3, replicas, 3, sources)),
            dma((2,)),
            dma((replicas, local)),
            dma((3, local)),
            dma((3, local)),
            dma((3, local)),
            dma((4, replicas, local)),
        ],
        compiler_params=pltpu.CompilerParams(
            collective_id=0, has_side_effects=True, vmem_limit_bytes=63 << 20
        ),
        name="gather_forward",
    )(inputs, out_grad, meta, weights.transpose(0, 2, 1, 3))


def by_collectives(inputs, out_grad, terms, mats, top, sources, half, swap):
    replicas = lax.axis_size("rep")
    me = lax.axis_index("rep")
    tok_dev = inputs.shape[0]
    local, part, width = mats.shape
    ffn = width // 3
    pair = 2 * ffn
    slots = sources * CAP
    meta = jnp.concatenate(terms).reshape(-1, part)
    meta_rows = meta.shape[0]
    pad = -meta_rows % 16
    meta = jnp.pad(meta, ((0, pad), (0, 0)))

    def arrive(q):
        at = (me ^ q) * part
        x = lax.dynamic_slice_in_dim(inputs, at, part, 1)
        g = lax.dynamic_slice_in_dim(out_grad, at, part, 1)
        return swap(jnp.concatenate([x, g, meta]), q)

    gathered = {}
    for start in range(replicas - half, -1, -half):
        chosen = range(start, start + half)
        block = jnp.stack([arrive(q) for q in reversed(chosen)])
        block = lax.all_gather(block, "exp", axis=0, tiled=False)
        for place, q in enumerate(reversed(chosen)):
            gathered[q] = block[:, place]

    mine = lax.axis_index("exp") * local + jnp.arange(local, dtype=jnp.int32)
    earlier = jnp.arange(tok_dev)[:, None] < jnp.arange(tok_dev)[None, :]
    base = (jnp.arange(sources) * CAP).astype(F32)
    pair_mats, down_mats = mats[..., :pair], mats[..., pair:]
    picks, rows_x, rows_g, arrivals = {}, {}, {}, {}
    for q in reversed(range(replicas)):
        if q == half - 1 and replicas > 1:
            later = {p: gathered[p] for p in range(half)}
            later, _ = lax.optimization_barrier((later, sent))
            gathered.update(later)
        got = gathered[q]
        info = got[:, 2 * tok_dev : 2 * tok_dev + meta_rows].astype(F32)
        info = info.reshape(sources, 4, top, tok_dev)
        weight = info[:, 1] + info[:, 2] + info[:, 3]
        hit = info[:, 0][None] == mine.astype(F32)[:, None, None, None]
        named = jnp.any(hit, axis=2)
        gate = jnp.sum(jnp.where(hit, weight[None], 0.0), axis=2)
        rank = jnp.einsum(
            "let,tu->leu", named.astype(BF16), earlier.astype(BF16), preferred_element_type=F32
        )
        rank = jnp.where(named, rank + base[None, :, None], -1.0)
        rank = rank.reshape(local, 1, sources * tok_dev)
        onehot = rank == jnp.arange(slots, dtype=F32)[None, :, None]
        gate = gate.reshape(local, 1, sources * tok_dev)
        gate_slot = jnp.sum(jnp.where(onehot, gate, 0.0), axis=2)
        picks[q] = onehot.astype(BF16)
        tokens_x = got[:, :tok_dev].reshape(sources * tok_dev, part)
        tokens_g = got[:, tok_dev : 2 * tok_dev].reshape(sources * tok_dev, part)
        x = jnp.einsum("lst,td->lsd", picks[q], tokens_x, preferred_element_type=F32)
        g = jnp.einsum("lst,td->lsd", picks[q], tokens_g, preferred_element_type=F32)
        rows_x[q] = x.astype(BF16)
        rows_g[q] = (g * gate_slot[..., None]).astype(BF16)
        hidden = jnp.einsum("lrd,ldh->lrh", rows_x[q], pair_mats, preferred_element_type=F32)
        da = jnp.einsum("lrd,ldh->lrh", rows_g[q], down_mats, preferred_element_type=F32)
        sums = [hidden, da]
        for term in arrivals.pop(q, []):
            sums = [old + new.astype(F32) for old, new in zip(sums, term)]
        sent = [one.astype(BF16) for one in sums]
        if q:
            arrivals.setdefault(q & (q - 1), []).append([swap(one, q & -q) for one in sent])

    hidden, da = sums
    hg, hu = hidden[..., :ffn], hidden[..., ffn:]
    sig = jax.nn.sigmoid(hg)
    act = (hg * sig * hu).astype(BF16)
    dhu = (da * hg * sig).astype(BF16)
    dhg = (da * hu * sig * (1.0 + hg * (1.0 - sig))).astype(BF16)
    d_pair, acts = {0: jnp.concatenate([dhg, dhu], axis=2)}, {0: act}
    for held in (d_pair, acts):
        bit = replicas // 2
        while bit:
            for q in list(held):
                held[q ^ bit] = swap(held[q], bit)
            bit //= 2

    def stacked(pieces):
        return jnp.stack([pieces[q] for q in range(replicas)])

    return stacked(rows_x), stacked(rows_g), stacked(d_pair), stacked(acts), picks


def per_device(inputs, out_grad, routes, gates, weights, moment_one, moment_two):
    replicas, sources = lax.axis_size("rep"), lax.axis_size("exp")
    tok_dev, top = routes.shape
    part, local, kinds, ffn = weights.shape
    pair = 2 * ffn
    slots = sources * CAP
    me = lax.axis_index("rep")

    def swap(array, bits):
        if bits == 0:
            return array
        return lax.ppermute(array, "rep", [(i, i ^ bits) for i in range(replicas)])

    terms, rest = [routes.astype(BF16).T], gates.T
    for _ in range(3):
        head = lax.reduce_precision(rest, 8, 7)
        terms.append(head.astype(BF16))
        rest = rest - head
    mats = weights.transpose(1, 0, 2, 3).reshape(local, part, kinds * ffn)
    pair_mats = mats[..., :pair]
    half = max(replicas // 2, 1)
    at_once = 2 * replicas * sources * tok_dev * part + 20 * local * slots * kinds * ffn
    if replicas == 4 and sources % 2 == 0 and at_once < 32 << 20:
        meta = jnp.concatenate(terms, axis=1)
        meta = jnp.pad(meta, ((0, -top % 16), (0, 0)))
        rows_x, rows_g, d_pair, acts, rank = forward(
            inputs, out_grad, meta, weights, replicas, sources, CAP
        )
        index = jnp.arange(slots, dtype=F32)[:, None]
        picks = [(rank[q][:, None, :] == index).astype(BF16) for q in range(replicas)]
    else:
        rows_x, rows_g, d_pair, acts, picks = by_collectives(
            inputs, out_grad, terms, mats, top, sources, half, swap
        )

    token_dx = {}
    for q in range(replicas):
        slot_dx = jnp.einsum(
            "lrh,ldh->lrd", d_pair[q], pair_mats, preferred_element_type=F32
        ).astype(BF16)
        dx = jnp.einsum("lst,lsd->td", picks[q], slot_dx, preferred_element_type=F32)
        token_dx[q] = dx.astype(BF16).reshape(sources, tok_dev, part)
    home = {}
    for start in range(0, replicas, half):
        block = jnp.concatenate([token_dx[q] for q in range(start, start + half)], axis=1)
        block = lax.psum_scatter(block, "exp", scatter_dimension=0, tiled=False)
        for place in range(half):
            one = block[place * tok_dev : (place + 1) * tok_dev]
            home[start + place] = swap(one, start + place)
    home = jnp.stack([home[q] for q in range(replicas)])
    input_grad = jnp.concatenate(
        [lax.dynamic_index_in_dim(home, me ^ q, 0, keepdims=False) for q in range(replicas)],
        axis=1,
    )

    first_moment, second_moment, new_weights = expert_update(
        rows_x, rows_g, d_pair, acts, weights, moment_one, moment_two
    )
    return (input_grad, first_moment, second_moment, new_weights)


def solution(mesh):
    tokens = P(("rep", "exp"), None)
    experts = P("rep", "exp", None, None)
    return jax.shard_map(
        per_device,
        mesh=mesh,
        in_specs=(tokens, tokens, tokens, tokens, experts, experts, experts),
        out_specs=(tokens, experts, experts, experts),
        check_vma=False,
    )
```

```python
import functools

import jax
import jax.numpy as jnp
from jax import lax
from jax.experimental import pallas as pl
from jax.experimental.pallas import tpu as pltpu
from jax.sharding import PartitionSpec as P


CAP = 18


beta_one = 0.9
beta_two = 0.95
learn_rate = 0.002
decay_rate = 0.1
epsilon = 1e-08
step_count = 100

F32 = jnp.float32
BF16 = jnp.bfloat16


MESH = pl.DeviceIdType.MESH


def flip(index, bits):
    for bit in (1, 2):
        if bits & bit:
            index = index + bit * (1 - 2 * ((index // bit) % 2))
    return index


class Scatter:
    def __init__(self, parts, sources, mine, theirs, refs):
        self.parts, self.mine, self.theirs = parts, mine, theirs
        self.from_side, self.from_z, self.total, self.home = refs[:4]
        self.y_send, self.y_got, self.z_send, self.z_got, self.h_send, self.h_got = refs[4:]
        self.me, self.ex = lax.axis_index("rep"), lax.axis_index("exp")
        self.col, self.z, self.line = self.ex % 2, self.ex // 2, sources // 2
        self.side = self.ex + 1 - 2 * self.col
        self.above, self.below = self.z + 1 < self.line, self.z >= 1

    def across(self, j, level):
        return pltpu.make_async_remote_copy(
            src_ref=self.theirs(j, level),
            dst_ref=self.from_side.at[j, level],
            send_sem=self.y_send.at[j, level],
            recv_sem=self.y_got.at[j, level],
            device_id={"exp": self.side},
            device_id_type=MESH,
        )

    def along(self, j, level, way):
        return pltpu.make_async_remote_copy(
            src_ref=self.mine(j, level),
            dst_ref=self.from_z.at[way, j, level],
            send_sem=self.z_send.at[way, j, level],
            recv_sem=self.z_got.at[way, j, level],
            device_id={"exp": self.ex + (2 if way == 0 else -2)},
            device_id_type=MESH,
        )

    def homeward(self, j):
        q = self.parts[j]
        if q == 0:
            return pltpu.make_async_copy(self.total.at[j], self.home.at[j], self.h_got.at[j])
        return pltpu.make_async_remote_copy(
            src_ref=self.total.at[j],
            dst_ref=self.home.at[j],
            send_sem=self.h_send.at[j],
            recv_sem=self.h_got.at[j],
            device_id={"rep": flip(self.me, q)},
            device_id_type=MESH,
        )

    def begin(self, j):
        for level in range(self.line):
            self.across(j, level).start()

    def add(self, j, level, ways, into):
        into[...] = sum(
            [self.from_z[way, j, level].astype(F32) for way in ways],
            self.mine(j, level)[...].astype(F32) + self.from_side[j, level].astype(F32),
        ).astype(BF16)

    def step(self, j, t):
        for way, level, near, fed in (
            (0, self.line - 1 - t, self.z < self.line - 1 - t, self.below),
            (1, t, self.z > t, self.above),
        ):

            @pl.when(near)
            def _():
                self.across(j, level).wait_recv()

                @pl.when(fed)
                def _():
                    self.along(j, level, way).wait_recv()
                    self.add(j, level, (way,), self.mine(j, level))

                @pl.when(jnp.logical_not(fed))
                def _():
                    self.add(j, level, (), self.mine(j, level))

                self.along(j, level, way).start()

    def finish(self, j):
        for level in range(self.line):

            @pl.when(self.z == level)
            def _():
                self.across(j, level).wait_recv()
                ways = [0] * (level >= 1) + [1] * (level + 1 < self.line)
                for way in ways:
                    self.along(j, level, way).wait_recv()
                self.add(j, level, ways, self.total.at[j])

        self.homeward(j).start()

    def end(self, j):
        if self.parts[j]:
            self.homeward(j).wait_recv()
            self.homeward(j).wait_send()
        else:
            self.homeward(j).wait()
        for level in range(self.line):
            self.across(j, level).wait_send()

            @pl.when(self.z < level)
            def _():
                self.along(j, level, 0).wait_send()

            @pl.when(self.z > level)
            def _():
                self.along(j, level, 1).wait_send()


def scatter_scratch(parts, sources, tok, part):
    line = sources // 2
    dma = pltpu.SemaphoreType.DMA
    return [
        pltpu.VMEM((parts, line, tok, part), BF16),
        pltpu.VMEM((2, parts, line, tok, part), BF16),
        pltpu.VMEM((parts, tok, part), BF16),
        pltpu.VMEM((parts, tok, part), BF16),
        dma((parts, line)),
        dma((parts, line)),
        dma((2, parts, line)),
        dma((2, parts, line)),
        dma((parts,)),
        dma((parts,)),
    ]


def update_kernel(dims, *refs):
    (replicas, slots, part, local, kinds, ffn, block, depth) = dims
    pieces, refs = refs[:4], refs[4:]
    m_one, m_two, w_in, o_one, o_two, w_out = refs[:6]
    bufs, (grad, b_one, b_two, b_w, in_sem, load_sem, store_sem) = refs[6:10], refs[10:]
    rows = replicas * slots
    twin = min(2, local)
    blocks = part // block
    ahead = min(depth, blocks)
    lanes = grad.shape[2]

    def fetch(e, go):
        for kind in range(4):
            for q in range(replicas):
                n = kind * replicas + q
                copy = pltpu.make_async_copy(
                    pieces[kind].at[q, e],
                    bufs[kind].at[lax.rem(e, twin), pl.ds(q * slots, slots)],
                    in_sem.at[lax.rem(e, twin), n],
                )
                copy.start() if go else copy.wait()

    def moves(i, outward):
        s = lax.rem(i, depth)
        part_of = pl.ds(i * block, block)
        if outward:
            trio = ((b_one, o_one), (b_two, o_two), (b_w, w_out))
            return [
                pltpu.make_async_copy(a.at[s], b.at[part_of], store_sem.at[n, s])
                for n, (a, b) in enumerate(trio)
            ]
        trio = ((b_one, m_one), (b_two, m_two), (b_w, w_in))
        return [
            pltpu.make_async_copy(b.at[part_of], a.at[s], load_sem.at[n, s])
            for n, (a, b) in enumerate(trio)
        ]

    fetch(0, True)

    @pl.loop(0, ahead)
    def _(i):
        for copy in moves(i, False):
            copy.start()

    @pl.loop(0, local)
    def _(e):
        if twin > 1:

            @pl.when(e + 1 < local)
            def _():
                fetch(e + 1, True)

        fetch(e, False)
        at = lax.rem(e, twin)
        base = pl.multiple_of(e * part, part)
        step = rows if rows <= 1024 else slots
        for lead, width, left, right in ((0, 2 * ffn, 0, 2), (2 * ffn, ffn, 1, 3)):
            for start in range(0, rows, step):
                one = lax.dot_general(
                    bufs[left][at, pl.ds(start, step), :],
                    bufs[right][at, pl.ds(start, step), :],
                    (((0,), (0,)), ((), ())),
                    preferred_element_type=F32,
                )
                for c in range(width // lanes):
                    tile = one[:, c * lanes : (c + 1) * lanes]
                    place = lead // lanes + c
                    if start:
                        tile = tile + grad[place, pl.ds(base, part), :]
                    grad[place, pl.ds(base, part), :] = tile

    correct_one = 1.0 - beta_one**step_count
    correct_two = 1.0 - beta_two**step_count

    def advance(i):
        s = lax.rem(i, depth)
        for copy in moves(i, False):
            copy.wait()

        @pl.loop(0, block // 4)
        def _(pair):
            spots = []
            for sub in range(4):
                row = pair * 4 + sub
                d = i * block + row
                of_d = pl.ds(d, local, stride=part) if local > 1 else pl.ds(d, 1)
                for place in range(kinds * ffn // lanes):
                    kind, c = divmod(place * lanes, ffn)
                    spots.append(((s, row, kind, slice(None), pl.ds(c, lanes)), place, of_d))
            held = [(b_one[at], b_two[at], b_w[at], grad[place, of_d, :]) for at, place, of_d in spots]
            done = []
            for one, two, w, g in held:
                first = beta_one * one + (1.0 - beta_one) * g
                second = beta_two * two + (1.0 - beta_two) * g * g
                w = w.astype(F32)
                root = jnp.sqrt(second * (1.0 / correct_two)) + epsilon
                update = first * (1.0 / correct_one) / root + decay_rate * w
                done.append((first, second, (w - learn_rate * update).astype(BF16)))
            for (at, _, _), (first, second, new) in zip(spots, done):
                b_one[at] = first
                b_two[at] = second
                b_w[at] = new

        for copy in moves(i, True):
            copy.start()

        @pl.when((i >= 1) & (i - 1 + depth < blocks))
        def _():
            for copy in moves(i - 1, True):
                copy.wait()
            for copy in moves(i - 1 + depth, False):
                copy.start()

    pl.loop(0, blocks)(advance)

    @pl.loop(max(blocks - depth, 0), blocks)
    def _(i):
        for copy in moves(i, True):
            copy.wait()


def expert_update(rows_x, rows_g, d_pair, acts, weights, moment_one, moment_two):
    replicas, local, slots, part = rows_x.shape
    kinds, ffn = weights.shape[2:]
    block = 32
    twin = min(2, local)
    rows = replicas * slots
    pieces = (rows_x, rows_g, d_pair, acts)
    held = [a.transpose(0, 2, 1, 3) for a in (moment_one, moment_two, weights)]
    depth = 10
    any_spec = pl.BlockSpec(memory_space=pl.ANY)
    out_shape = tuple(jax.ShapeDtypeStruct(a.shape, a.dtype) for a in held)
    kernel = functools.partial(
        update_kernel, (replicas, slots, part, local, kinds, ffn, block, depth)
    )
    outs = pl.pallas_call(
        kernel,
        out_shape=out_shape,
        in_specs=[any_spec] * (len(pieces) + 3),
        out_specs=(any_spec,) * len(out_shape),
        scratch_shapes=[
            pltpu.VMEM((twin, rows, part), BF16),
            pltpu.VMEM((twin, rows, part), BF16),
            pltpu.VMEM((twin, rows, 2 * ffn), BF16),
            pltpu.VMEM((twin, rows, ffn), BF16),
            pltpu.VMEM((kinds * ffn // 128, local * part, 128), F32),
            pltpu.VMEM((depth, block, kinds, local, ffn), F32),
            pltpu.VMEM((depth, block, kinds, local, ffn), F32),
            pltpu.VMEM((depth, block, kinds, local, ffn), BF16),
            pltpu.SemaphoreType.DMA((twin, 4 * replicas)),
            pltpu.SemaphoreType.DMA((3, depth)),
            pltpu.SemaphoreType.DMA((3, depth)),
        ],
        compiler_params=pltpu.CompilerParams(vmem_limit_bytes=60 << 20),
        cost_estimate=pl.CostEstimate(
            flops=2 * rows * part * kinds * ffn * local,
            bytes_accessed=2 * sum(a.size * a.dtype.itemsize for a in held),
            transcendentals=0,
        ),
        name="expert_update",
    )(*pieces, *held)
    return [a.transpose(0, 2, 1, 3) for a in outs]


def forward_kernel(dims, x, g, meta, weights, out_x, out_g, out_pair, out_act, out_dx, out_home, *scratch):
    replicas, sources, tok, part, local, slots, ffn, cap = dims
    (gx, gg, gm, w, rank, gate, rows_x, rows_g, outgoing, incoming, own, held, raw, turned) = scratch[:14]
    sum_dx, scratch = scratch[14], scratch[15:]
    (own_send, got, sent, w_sem, part_send, part_got, d_send, d_got, out_sem, row_sem) = scratch[:10]
    scatter_refs = scratch[10:]
    ring = rows_x.shape[0]
    me, ex = lax.axis_index("rep"), lax.axis_index("exp")
    col, z = ex % 2, ex // 2
    line = sources // 2
    side = ex + 1 - 2 * col
    above, below = z + 1 < line, z >= 1
    pair = 2 * ffn
    order = tuple(reversed(range(replicas)))
    kinds = ((gm, meta), (gx, x), (gg, g))

    barrier = pltpu.get_barrier_semaphore()
    for q in order[:-1]:
        pl.semaphore_signal(barrier, inc=1, device_id={"rep": flip(me, q)}, device_id_type=MESH)
    pl.semaphore_signal(barrier, inc=1, device_id={"exp": side}, device_id_type=MESH)

    @pl.when(above)
    def _():
        pl.semaphore_signal(barrier, inc=1, device_id={"exp": ex + 2}, device_id_type=MESH)

    @pl.when(below)
    def _():
        pl.semaphore_signal(barrier, inc=1, device_id={"exp": ex - 2}, device_id_type=MESH)

    lanes = turned.shape[2]
    chunk = raw.shape[1]
    chunks = part // chunk

    def load_w(c):
        return pltpu.make_async_copy(
            weights.at[pl.ds(c * chunk, chunk)], raw.at[c % 2], w_sem.at[c % 2]
        )

    def turn(c):
        if c + 1 < chunks:
            load_w(c + 1).start()
        load_w(c).wait()
        unroll = 4

        @pl.loop(0, chunk // unroll)
        def _(d4):
            for sub in range(unroll):
                d = d4 * unroll + sub
                for place in range(3 * ffn // lanes):
                    kind, at = divmod(place * lanes, ffn)
                    tile = raw[c % 2, d, kind, :, pl.ds(at, lanes)].astype(F32)
                    turned[place, pl.ds(d, local, stride=chunk), :] = tile

        @pl.loop(0, local)
        def _(l):
            for place in range(3 * ffn // lanes):
                tile = turned[place, pl.ds(pl.multiple_of(l * chunk, chunk), chunk), :]
                w[l, pl.ds(c * chunk, chunk), pl.ds(place * lanes, lanes)] = tile.astype(BF16)

    load_w(0).start()
    expected = replicas + jnp.where(above, 1, 0) + jnp.where(below, 1, 0)
    pl.semaphore_wait(barrier, expected)

    def first(q, n):
        buf, src = kinds[n]
        target = flip(me, q)
        if n:
            src = src.at[:, pl.ds(pl.multiple_of(target * part, part), part)]
        if q == 0:
            return pltpu.make_async_copy(src, buf.at[q, ex], got.at[q, n, ex])
        return pltpu.make_async_remote_copy(
            src_ref=src,
            dst_ref=buf.at[q, ex],
            send_sem=own_send.at[q, n],
            recv_sem=got.at[q, n, ex],
            device_id={"rep": target},
            device_id_type=MESH,
        )

    def hop(q, n, slot, way):
        target = (side, ex + 2, ex - 2)[way]
        return pltpu.make_async_remote_copy(
            src_ref=kinds[n][0].at[q, slot],
            dst_ref=kinds[n][0].at[q, slot],
            send_sem=sent.at[way, q, n, slot],
            recv_sem=got.at[q, n, slot],
            device_id={"exp": target},
            device_id_type=MESH,
        )

    for q in order:
        for n in range(3):
            first(q, n).start()

    def relay(q, step):
        for n in range(3):
            if step == 0:
                if q:
                    first(q, n).wait_recv()
                else:
                    first(q, n).wait()
                hop(q, n, ex, 0).start()

                @pl.when(above)
                def _():
                    hop(q, n, ex, 1).start()

                @pl.when(below)
                def _():
                    hop(q, n, ex, 2).start()

                continue

            @pl.when(z >= step)
            def _():
                slot = ex - 2 * step
                hop(q, n, slot, 0).wait_recv()
                hop(q, n, slot, 0).start()

                @pl.when(above)
                def _():
                    hop(q, n, slot, 1).start()

            @pl.when(z + step < line)
            def _():
                slot = ex + 2 * step
                hop(q, n, slot, 0).wait_recv()
                hop(q, n, slot, 0).start()

                @pl.when(below)
                def _():
                    hop(q, n, slot, 2).start()

    def settle(q):
        for n in range(3):
            for level in range(line):
                hop(q, n, 2 * level + 1 - col, 0).wait_recv()

    lower = lax.broadcasted_iota(jnp.int32, (tok, tok), 0)
    upper = lax.broadcasted_iota(jnp.int32, (tok, tok), 1)
    earlier = jnp.where(lower < upper, 1.0, 0.0).astype(BF16)
    expert0 = (ex * local).astype(F32)

    def prepare(q):
        @pl.loop(0, sources)
        def _(s):
            info = gm[q, s].astype(F32)[:8]
            routes = info[:, :tok]
            weight = info[:, tok : 2 * tok] + info[:, 2 * tok : 3 * tok] + info[:, 3 * tok :]
            named, gates = [], []
            for l in range(local):
                hit = routes == expert0 + l
                named.append(jnp.max(jnp.where(hit, 1.0, 0.0), axis=0, keepdims=True))
                gates.append(jnp.sum(jnp.where(hit, weight, 0.0), axis=0, keepdims=True))
            named = jnp.concatenate(named, axis=0)
            places = jnp.dot(named.astype(BF16), earlier, preferred_element_type=F32)
            places = jnp.where(named > 0.0, places + (s * cap).astype(F32), -1.0)
            at = pl.ds(pl.multiple_of(s * tok, tok), tok)
            rank[q, :, at] = places
            gate[:, at] = jnp.concatenate(gates, axis=0)

    def exchange(l, q):
        slot, into, bits = {3: (0, 0, 1), 2: (1, 2, 2), 1: (0, 1, 1)}[q]
        return pltpu.make_async_remote_copy(
            src_ref=outgoing.at[slot, l],
            dst_ref=incoming.at[into, l],
            send_sem=part_send.at[q, l],
            recv_sem=part_got.at[into, l],
            device_id={"rep": flip(me, bits)},
            device_id_type=MESH,
        )

    def row_out(l, q):
        slot = (l + (replicas - 1 - q) * local) % ring
        return (
            pltpu.make_async_copy(rows_x.at[slot], out_x.at[q, l], row_sem.at[0, slot]),
            pltpu.make_async_copy(rows_g.at[slot], out_g.at[q, l], row_sem.at[1, slot]),
        )

    def piece(l, q):
        places = rank[q, pl.ds(l, 1), :]
        index = lax.broadcasted_iota(jnp.int32, (slots, sources * tok), 0).astype(F32)
        hit = index == places
        pick = jnp.where(hit, 1.0, 0.0).astype(BF16)
        gates = jnp.sum(jnp.where(hit, gate[pl.ds(l, 1), :], 0.0), axis=1, keepdims=True)
        tokens_x = gx[q].reshape(sources * tok, part)
        tokens_g = gg[q].reshape(sources * tok, part)
        rx = jnp.dot(pick, tokens_x, preferred_element_type=F32).astype(BF16)
        rg = (jnp.dot(pick, tokens_g, preferred_element_type=F32) * gates).astype(BF16)
        turn_of = l + (replicas - 1 - q) * local
        slot = turn_of % ring

        @pl.when(turn_of >= ring)
        def _():
            for copy in row_out(l, q):
                copy.wait()

        rows_x[slot] = rx
        rows_g[slot] = rg
        for copy in row_out(l, q):
            copy.start()
        hidden = jnp.dot(rx, w[l, :, :pair], preferred_element_type=F32)
        da = jnp.dot(rg, w[l, :, pair:], preferred_element_type=F32)
        for lead, width, one in ((0, pair, hidden), (pair, ffn, da)):
            at = pl.ds(lead, width)
            if q == 3:
                outgoing[0, l, :, at] = one.astype(BF16)
            elif q == 2:
                if not lead:
                    exchange(l, 3).wait_recv()
                outgoing[1, l, :, at] = (one + incoming[0, l, :, at].astype(F32)).astype(BF16)
            elif q == 1:
                if not lead:
                    exchange(l, 3).wait_send()
                outgoing[0, l, :, at] = one.astype(BF16)
            else:
                if not lead:
                    exchange(l, 1).wait_recv()
                own[l, :, at] = one + incoming[1, l, :, at].astype(F32)
        if q:
            exchange(l, q).start()

    def grads_to(l, way):
        src, dst, bits = ((0, 1, 1), (0, 2, 2), (2, 3, 1))[way]
        return pltpu.make_async_remote_copy(
            src_ref=held.at[src, l],
            dst_ref=held.at[dst, l],
            send_sem=d_send.at[way, l],
            recv_sem=d_got.at[way, l],
            device_id={"rep": flip(me, bits)},
            device_id_type=MESH,
        )

    def d_out(l, q):
        return (
            pltpu.make_async_copy(
                held.at[q, l, :, pl.ds(0, pair)], out_pair.at[q, l], out_sem.at[0, q, l]
            ),
            pltpu.make_async_copy(
                held.at[q, l, :, pl.ds(pair, ffn)], out_act.at[q, l], out_sem.at[1, q, l]
            ),
        )

    def finish(l):
        exchange(l, 2).wait_recv()
        sums = [
            own[l, :, pl.ds(n * ffn, ffn)] + incoming[2, l, :, pl.ds(n * ffn, ffn)].astype(F32)
            for n in range(3)
        ]
        hg, hu, da = sums
        sig = jax.nn.sigmoid(hg)
        held[0, l, :, pl.ds(2 * ffn, ffn)] = (hg * sig * hu).astype(BF16)
        held[0, l, :, pl.ds(ffn, ffn)] = (da * hg * sig).astype(BF16)
        held[0, l, :, pl.ds(0, ffn)] = (da * hu * sig * (1.0 + hg * (1.0 - sig))).astype(BF16)
        for way in (1, 0):
            grads_to(l, way).start()
        for copy in d_out(l, 0):
            copy.start()

    def pass_on(l):
        grads_to(l, 1).wait_recv()
        grads_to(l, 2).start()
        for copy in d_out(l, 2):
            copy.start()

    def pieces(lo, hi, q):
        @pl.loop(lo, hi)
        def _(l):
            piece(l, q)

    steps = max(line - 1, 1)
    turns = [range(chunks * n // (steps + 1), chunks * (n + 1) // (steps + 1)) for n in range(steps + 1)]
    for c in turns[0]:
        turn(c)
    relay(order[0], 0)
    for i, q in enumerate(order):
        if i + 1 < replicas:
            relay(order[i + 1], 0)
        for step in range(1, line):
            relay(q, step)
            if not i:
                for c in turns[step]:
                    turn(c)
            if i:
                pieces(local * (step - 1) // steps, local * step // steps, order[i - 1])
        settle(q)
        prepare(q)

    @pl.loop(0, local)
    def _(l):
        piece(l, order[-1])
        finish(l)

    def sent_blocks(q, n):
        @pl.loop(0, line)
        def _(level):
            slot = 2 * level + col
            hop(q, n, slot, 0).wait_send()

            @pl.when(above & (level <= z))
            def _():
                hop(q, n, slot, 1).wait_send()

            @pl.when(below & (level >= z))
            def _():
                hop(q, n, slot, 2).wait_send()

    def add_dx(l, q, total):
        hit = lax.broadcasted_iota(jnp.int32, (slots, sources * tok), 0).astype(F32)
        pick = jnp.where(hit == rank[q, pl.ds(l, 1), :], 1.0, 0.0).astype(BF16)
        slot_dx = lax.dot_general(
            held[q, l, :, :pair],
            w[l, :, :pair],
            (((1,), (1,)), ((), ())),
            preferred_element_type=F32,
        ).astype(BF16)
        sum_dx[total] += lax.dot_general(
            pick, slot_dx, (((0,), (0,)), ((), ())), preferred_element_type=F32
        )

    def round_dx(q, total):
        sent_blocks(q, 1)
        gx[q] = sum_dx[total].reshape(sources, tok, part).astype(BF16)

    near = Scatter(
        (0, 1),
        sources,
        lambda j, level: gx.at[j, 2 * level + col],
        lambda j, level: gx.at[j, 2 * level + 1 - col],
        scatter_refs,
    )
    sum_dx[...] = jnp.zeros_like(sum_dx)

    @pl.loop(0, local)
    def _(l):
        add_dx(l, 0, 0)

    round_dx(0, 0)
    near.begin(0)

    @pl.loop(0, local)
    def _(l):
        grads_to(l, 0).wait_recv()
        for copy in d_out(l, 1):
            copy.start()
        add_dx(l, 1, 1)

    round_dx(1, 1)
    near.begin(1)
    sum_dx[...] = jnp.zeros_like(sum_dx)
    for t in range(line - 1):
        for j in range(2):
            near.step(j, t)
    for j in range(2):
        near.finish(j)

    @pl.loop(0, local + 1)
    def _(l):
        @pl.when(l < local)
        def _():
            pass_on(l)
            add_dx(l, 2, 0)

        @pl.when(l >= 1)
        def _():
            grads_to(l - 1, 2).wait_recv()
            for copy in d_out(l - 1, 3):
                copy.start()
            add_dx(l - 1, 3, 1)

    last = []
    for q in (2, 3):
        round_dx(q, q - 2)
        last.append(pltpu.make_async_copy(gx.at[q], out_dx.at[:, q - 2], w_sem.at[q - 2]))
        last[-1].start()
    for j in range(2):
        near.end(j)
    home_copy = pltpu.make_async_copy(near.home, out_home, own_send.at[0, 0])
    home_copy.start()

    @pl.loop(0, local)
    def _(l):
        for q in (2, 1):
            exchange(l, q).wait_send()
        for way in range(3):
            grads_to(l, way).wait_send()
        for q in range(replicas):
            for copy in d_out(l, q):
                copy.wait()

        @pl.when(l >= local - ring)
        def _():
            for copy in row_out(l, 0):
                copy.wait()

    for q in order:
        for n in range(3):
            if q:
                first(q, n).wait_send()
            if n != 1:
                sent_blocks(q, n)
    for copy in (*last, home_copy):
        copy.wait()


def forward(inputs, out_grad, meta, weights, replicas, sources, cap):
    tok = inputs.shape[0]
    part, local, kinds, ffn = weights.shape
    width = kinds * ffn
    chunk = part // 16
    ring = min(4, local)
    slots = sources * cap
    dims = (replicas, sources, tok, part, local, slots, ffn, cap)
    any_spec = pl.BlockSpec(memory_space=pl.ANY)
    rows = (replicas, local, slots)
    dma = pltpu.SemaphoreType.DMA
    return pl.pallas_call(
        functools.partial(forward_kernel, dims),
        out_shape=(
            jax.ShapeDtypeStruct((*rows, part), BF16),
            jax.ShapeDtypeStruct((*rows, part), BF16),
            jax.ShapeDtypeStruct((*rows, 2 * ffn), BF16),
            jax.ShapeDtypeStruct((*rows, ffn), BF16),
            jax.ShapeDtypeStruct((sources, 2, tok, part), BF16),
            jax.ShapeDtypeStruct((2, tok, part), BF16),
        ),
        in_specs=[any_spec] * 4,
        out_specs=(any_spec,) * 6,
        scratch_shapes=[
            pltpu.VMEM((replicas, sources, tok, part), BF16),
            pltpu.VMEM((replicas, sources, tok, part), BF16),
            pltpu.VMEM((replicas, sources, *meta.shape), BF16),
            pltpu.VMEM((local, part, width), BF16),
            pltpu.VMEM((replicas, local, sources * tok), F32),
            pltpu.VMEM((local, sources * tok), F32),
            pltpu.VMEM((ring, slots, part), BF16),
            pltpu.VMEM((ring, slots, part), BF16),
            pltpu.VMEM((2, local, slots, width), BF16),
            pltpu.VMEM((3, local, slots, width), BF16),
            pltpu.VMEM((local, slots, width), F32),
            pltpu.VMEM((*rows, width), BF16),
            pltpu.VMEM((2, chunk, kinds, local, ffn), BF16),
            pltpu.VMEM((width // 128, local * chunk, 128), F32),
            pltpu.VMEM((2, sources * tok, part), F32),
            dma((replicas, 3)),
            dma((replicas, 3, sources)),
            dma((3, replicas, 3, sources)),
            dma((2,)),
            dma((replicas, local)),
            dma((3, local)),
            dma((3, local)),
            dma((3, local)),
            dma((2, replicas, local)),
            dma((2, ring)),
            *scatter_scratch(2, sources, tok, part),
        ],
        compiler_params=pltpu.CompilerParams(
            collective_id=0, has_side_effects=True, vmem_limit_bytes=63 << 20
        ),
        name="gather_forward",
    )(inputs, out_grad, meta, weights.transpose(0, 2, 1, 3))


def by_collectives(inputs, out_grad, terms, weights, top, sources, swap):
    replicas = lax.axis_size("rep")
    me = lax.axis_index("rep")
    tok_dev = inputs.shape[0]
    part, local, kinds, ffn = weights.shape
    pair = 2 * ffn
    slots = sources * CAP
    half = max(replicas // 2, 1)
    mats = weights.transpose(1, 0, 2, 3).reshape(local, part, kinds * ffn)
    meta = jnp.concatenate(terms).reshape(-1, part)
    meta_rows = meta.shape[0]
    pad = -meta_rows % 16
    meta = jnp.pad(meta, ((0, pad), (0, 0)))

    def arrive(q):
        at = (me ^ q) * part
        x = lax.dynamic_slice_in_dim(inputs, at, part, 1)
        g = lax.dynamic_slice_in_dim(out_grad, at, part, 1)
        return swap(jnp.concatenate([x, g, meta]), q)

    gathered = {}
    for start in range(replicas - half, -1, -half):
        chosen = range(start, start + half)
        block = jnp.stack([arrive(q) for q in reversed(chosen)])
        block = lax.all_gather(block, "exp", axis=0, tiled=False)
        for place, q in enumerate(reversed(chosen)):
            gathered[q] = block[:, place]

    mine = lax.axis_index("exp") * local + jnp.arange(local, dtype=jnp.int32)
    earlier = jnp.arange(tok_dev)[:, None] < jnp.arange(tok_dev)[None, :]
    base = (jnp.arange(sources) * CAP).astype(F32)
    pair_mats, down_mats = mats[..., :pair], mats[..., pair:]
    picks, rows_x, rows_g, arrivals = {}, {}, {}, {}
    for q in reversed(range(replicas)):
        if q == half - 1 and replicas > 1:
            later = {p: gathered[p] for p in range(half)}
            later, _ = lax.optimization_barrier((later, sent))
            gathered.update(later)
        got = gathered[q]
        info = got[:, 2 * tok_dev : 2 * tok_dev + meta_rows].astype(F32)
        info = info.reshape(sources, 4, top, tok_dev)
        weight = info[:, 1] + info[:, 2] + info[:, 3]
        hit = info[:, 0][None] == mine.astype(F32)[:, None, None, None]
        named = jnp.any(hit, axis=2)
        gate = jnp.sum(jnp.where(hit, weight[None], 0.0), axis=2)
        rank = jnp.einsum(
            "let,tu->leu", named.astype(BF16), earlier.astype(BF16), preferred_element_type=F32
        )
        rank = jnp.where(named, rank + base[None, :, None], -1.0)
        rank = rank.reshape(local, 1, sources * tok_dev)
        onehot = rank == jnp.arange(slots, dtype=F32)[None, :, None]
        gate = gate.reshape(local, 1, sources * tok_dev)
        gate_slot = jnp.sum(jnp.where(onehot, gate, 0.0), axis=2)
        picks[q] = onehot.astype(BF16)
        tokens_x = got[:, :tok_dev].reshape(sources * tok_dev, part)
        tokens_g = got[:, tok_dev : 2 * tok_dev].reshape(sources * tok_dev, part)
        x = jnp.einsum("lst,td->lsd", picks[q], tokens_x, preferred_element_type=F32)
        g = jnp.einsum("lst,td->lsd", picks[q], tokens_g, preferred_element_type=F32)
        rows_x[q] = x.astype(BF16)
        rows_g[q] = (g * gate_slot[..., None]).astype(BF16)
        hidden = jnp.einsum("lrd,ldh->lrh", rows_x[q], pair_mats, preferred_element_type=F32)
        da = jnp.einsum("lrd,ldh->lrh", rows_g[q], down_mats, preferred_element_type=F32)
        sums = [hidden, da]
        for term in arrivals.pop(q, []):
            sums = [old + new.astype(F32) for old, new in zip(sums, term)]
        sent = [one.astype(BF16) for one in sums]
        if q:
            arrivals.setdefault(q & (q - 1), []).append([swap(one, q & -q) for one in sent])

    hidden, da = sums
    hg, hu = hidden[..., :ffn], hidden[..., ffn:]
    sig = jax.nn.sigmoid(hg)
    act = (hg * sig * hu).astype(BF16)
    dhu = (da * hg * sig).astype(BF16)
    dhg = (da * hu * sig * (1.0 + hg * (1.0 - sig))).astype(BF16)
    d_pair, acts = {0: jnp.concatenate([dhg, dhu], axis=2)}, {0: act}
    for held in (d_pair, acts):
        bit = replicas // 2
        while bit:
            for q in list(held):
                held[q ^ bit] = swap(held[q], bit)
            bit //= 2

    token_dx = {}
    for q in range(replicas):
        slot_dx = jnp.einsum(
            "lrh,ldh->lrd", d_pair[q], pair_mats, preferred_element_type=F32
        ).astype(BF16)
        dx = jnp.einsum("lst,lsd->td", picks[q], slot_dx, preferred_element_type=F32)
        token_dx[q] = dx.astype(BF16).reshape(sources, tok_dev, part)
    home = {}
    for start in range(0, replicas, half):
        block = jnp.concatenate([token_dx[q] for q in range(start, start + half)], axis=1)
        block = lax.psum_scatter(block, "exp", scatter_dimension=0, tiled=False)
        for place in range(half):
            one = block[place * tok_dev : (place + 1) * tok_dev]
            home[start + place] = swap(one, start + place)
    home = jnp.stack([home[q] for q in range(replicas)])

    def stacked(pieces):
        return jnp.stack([pieces[q] for q in range(replicas)])

    return stacked(rows_x), stacked(rows_g), stacked(d_pair), stacked(acts), home


def per_device(inputs, out_grad, routes, gates, weights, moment_one, moment_two):
    replicas, sources = lax.axis_size("rep"), lax.axis_size("exp")
    tok_dev, top = routes.shape
    part, local, kinds, ffn = weights.shape
    slots = sources * CAP
    me = lax.axis_index("rep")

    def swap(array, bits):
        if bits == 0:
            return array
        return lax.ppermute(array, "rep", [(i, i ^ bits) for i in range(replicas)])

    terms, rest = [routes.astype(BF16).T], gates.T
    for _ in range(3):
        head = lax.reduce_precision(rest, 8, 7)
        terms.append(head.astype(BF16))
        rest = rest - head
    at_once = 2 * replicas * sources * tok_dev * part + 20 * local * slots * kinds * ffn
    if replicas == 4 and sources % 2 == 0 and at_once < 32 << 20:
        meta = jnp.concatenate(terms, axis=1)
        meta = jnp.pad(meta, ((0, -top % 16), (0, 0)))
        *grown, dx, near = forward(inputs, out_grad, meta, weights, replicas, sources, CAP)
        far = lax.psum_scatter(
            dx.reshape(sources, 2 * tok_dev, part), "exp", scatter_dimension=0, tiled=False
        )
        far = [swap(far[j * tok_dev : (j + 1) * tok_dev], j + 2) for j in range(2)]
        first_moment, second_moment, new_weights = expert_update(
            *grown, weights, moment_one, moment_two
        )
        home = jnp.concatenate([near, jnp.stack(far)])
    else:
        *grown, home = by_collectives(inputs, out_grad, terms, weights, top, sources, swap)
        first_moment, second_moment, new_weights = expert_update(
            *grown, weights, moment_one, moment_two
        )
    input_grad = jnp.concatenate(
        [lax.dynamic_index_in_dim(home, me ^ q, 0, keepdims=False) for q in range(replicas)],
        axis=1,
    )
    return (input_grad, first_moment, second_moment, new_weights)


def solution(mesh):
    tokens = P(("rep", "exp"), None)
    experts = P("rep", "exp", None, None)
    return jax.shard_map(
        per_device,
        mesh=mesh,
        in_specs=(tokens, tokens, tokens, tokens, experts, experts, experts),
        out_specs=(tokens, experts, experts, experts),
        check_vma=False,
    )
```

```python
import functools

import jax
import jax.numpy as jnp
from jax import lax
from jax.experimental import pallas as pl
from jax.experimental.pallas import tpu as pltpu
from jax.sharding import PartitionSpec as P


CAP = 18


beta_one = 0.9
beta_two = 0.95
learn_rate = 0.002
decay_rate = 0.1
epsilon = 1e-08
step_count = 100

F32 = jnp.float32
BF16 = jnp.bfloat16


MESH = pl.DeviceIdType.MESH


def flip(index, bits):
    for place in range(bits.bit_length()):
        bit = 1 << place
        if bits & bit:
            index = index + bit * (1 - 2 * ((index // bit) % 2))
    return index


class Scatter:
    def __init__(self, parts, sources, mine, theirs, refs):
        self.parts, self.mine, self.theirs = parts, mine, theirs
        self.from_side, self.from_z, self.total, self.home = refs[:4]
        self.y_send, self.y_got, self.z_send, self.z_got, self.h_send, self.h_got = refs[4:]
        self.me, self.ex = lax.axis_index("rep"), lax.axis_index("exp")
        self.col, self.z, self.line = self.ex % 2, self.ex // 2, sources // 2
        self.side = self.ex + 1 - 2 * self.col
        self.above, self.below = self.z + 1 < self.line, self.z >= 1

    def across(self, j, level):
        return pltpu.make_async_remote_copy(
            src_ref=self.theirs(j, level),
            dst_ref=self.from_side.at[j, level],
            send_sem=self.y_send.at[j, level],
            recv_sem=self.y_got.at[j, level],
            device_id={"exp": self.side},
            device_id_type=MESH,
        )

    def along(self, j, level, way):
        return pltpu.make_async_remote_copy(
            src_ref=self.mine(j, level),
            dst_ref=self.from_z.at[way, j, level],
            send_sem=self.z_send.at[way, j, level],
            recv_sem=self.z_got.at[way, j, level],
            device_id={"exp": self.ex + (2 if way == 0 else -2)},
            device_id_type=MESH,
        )

    def homeward(self, j):
        q = self.parts[j]
        if q == 0:
            return pltpu.make_async_copy(self.total.at[j], self.home.at[j], self.h_got.at[j])
        return pltpu.make_async_remote_copy(
            src_ref=self.total.at[j],
            dst_ref=self.home.at[j],
            send_sem=self.h_send.at[j],
            recv_sem=self.h_got.at[j],
            device_id={"rep": flip(self.me, q)},
            device_id_type=MESH,
        )

    def begin(self, j):
        for t in range((self.line + 1) // 2):
            for level in sorted({self.line - 1 - t, t}, reverse=True):
                self.across(j, level).start()

    def add(self, j, level, ways, into):
        into[...] = sum(
            [self.from_z[way, j, level].astype(F32) for way in ways],
            self.mine(j, level)[...].astype(F32) + self.from_side[j, level].astype(F32),
        ).astype(BF16)

    def step(self, j, t):
        for way, level, near, fed in (
            (0, self.line - 1 - t, self.z < self.line - 1 - t, self.below),
            (1, t, self.z > t, self.above),
        ):

            @pl.when(near)
            def _():
                self.across(j, level).wait_recv()

                @pl.when(fed)
                def _():
                    self.along(j, level, way).wait_recv()
                    self.add(j, level, (way,), self.mine(j, level))

                @pl.when(jnp.logical_not(fed))
                def _():
                    self.add(j, level, (), self.mine(j, level))

                self.along(j, level, way).start()

    def finish(self, j):
        for level in range(self.line):

            @pl.when(self.z == level)
            def _():
                self.across(j, level).wait_recv()
                ways = [0] * (level >= 1) + [1] * (level + 1 < self.line)
                for way in ways:
                    self.along(j, level, way).wait_recv()
                self.add(j, level, ways, self.total.at[j])

        self.homeward(j).start()

    def end(self, j):
        if self.parts[j]:
            self.homeward(j).wait_recv()
            self.homeward(j).wait_send()
        else:
            self.homeward(j).wait()
        for level in range(self.line):
            self.across(j, level).wait_send()

            @pl.when(self.z < level)
            def _():
                self.along(j, level, 0).wait_send()

            @pl.when(self.z > level)
            def _():
                self.along(j, level, 1).wait_send()


def scatter_scratch(parts, sources, tok, part):
    line = sources // 2
    dma = pltpu.SemaphoreType.DMA
    return [
        pltpu.VMEM((parts, line, tok, part), BF16),
        pltpu.VMEM((2, parts, line, tok, part), BF16),
        pltpu.VMEM((parts, tok, part), BF16),
        pltpu.VMEM((parts, tok, part), BF16),
        dma((parts, line)),
        dma((parts, line)),
        dma((2, parts, line)),
        dma((2, parts, line)),
        dma((parts,)),
        dma((parts,)),
    ]


def update_kernel(dims, *refs):
    (replicas, slots, part, local, kinds, ffn, block, depth) = dims
    pieces, refs = refs[:4], refs[4:]
    m_one, m_two, w_in, o_one, o_two, w_out = refs[:6]
    bufs, (grad, b_one, b_two, b_w, in_sem, load_sem, store_sem) = refs[6:10], refs[10:]
    rows = replicas * slots
    twin = min(2, local)
    blocks = part // block
    ahead = min(depth, blocks)
    lanes = grad.shape[2]

    def fetch(e, go):
        for kind in range(4):
            for q in range(replicas):
                n = kind * replicas + q
                copy = pltpu.make_async_copy(
                    pieces[kind].at[q, e],
                    bufs[kind].at[lax.rem(e, twin), pl.ds(q * slots, slots)],
                    in_sem.at[lax.rem(e, twin), n],
                )
                copy.start() if go else copy.wait()

    def moves(i, outward):
        s = lax.rem(i, depth)
        part_of = pl.ds(i * block, block)
        if outward:
            trio = ((b_one, o_one), (b_two, o_two), (b_w, w_out))
            return [
                pltpu.make_async_copy(a.at[s], b.at[part_of], store_sem.at[n, s])
                for n, (a, b) in enumerate(trio)
            ]
        trio = ((b_one, m_one), (b_two, m_two), (b_w, w_in))
        return [
            pltpu.make_async_copy(b.at[part_of], a.at[s], load_sem.at[n, s])
            for n, (a, b) in enumerate(trio)
        ]

    fetch(0, True)

    @pl.loop(0, ahead)
    def _(i):
        for copy in moves(i, False):
            copy.start()

    @pl.loop(0, local)
    def _(e):
        if twin > 1:

            @pl.when(e + 1 < local)
            def _():
                fetch(e + 1, True)

        fetch(e, False)
        at = lax.rem(e, twin)
        base = pl.multiple_of(e * part, part)
        step = rows if rows <= 1024 else slots
        for lead, width, left, right in ((0, 2 * ffn, 0, 2), (2 * ffn, ffn, 1, 3)):
            for start in range(0, rows, step):
                one = lax.dot_general(
                    bufs[left][at, pl.ds(start, step), :],
                    bufs[right][at, pl.ds(start, step), :],
                    (((0,), (0,)), ((), ())),
                    preferred_element_type=F32,
                )
                for c in range(width // lanes):
                    tile = one[:, c * lanes : (c + 1) * lanes]
                    place = lead // lanes + c
                    if start:
                        tile = tile + grad[place, pl.ds(base, part), :]
                    grad[place, pl.ds(base, part), :] = tile

    correct_one = 1.0 - beta_one**step_count
    correct_two = 1.0 - beta_two**step_count

    def advance(i):
        s = lax.rem(i, depth)
        for copy in moves(i, False):
            copy.wait()

        @pl.loop(0, block // 4)
        def _(pair):
            spots = []
            for sub in range(4):
                row = pair * 4 + sub
                d = i * block + row
                of_d = pl.ds(d, local, stride=part) if local > 1 else pl.ds(d, 1)
                for place in range(kinds * ffn // lanes):
                    kind, c = divmod(place * lanes, ffn)
                    spots.append(((s, row, kind, slice(None), pl.ds(c, lanes)), place, of_d))
            held = [(b_one[at], b_two[at], b_w[at], grad[place, of_d, :]) for at, place, of_d in spots]
            done = []
            for one, two, w, g in held:
                first = beta_one * one + (1.0 - beta_one) * g
                second = beta_two * two + (1.0 - beta_two) * g * g
                w = w.astype(F32)
                root = jnp.sqrt(second * (1.0 / correct_two)) + epsilon
                update = first * (1.0 / correct_one) / root + decay_rate * w
                done.append((first, second, (w - learn_rate * update).astype(BF16)))
            for (at, _, _), (first, second, new) in zip(spots, done):
                b_one[at] = first
                b_two[at] = second
                b_w[at] = new

        for copy in moves(i, True):
            copy.start()

        @pl.when((i >= 1) & (i - 1 + depth < blocks))
        def _():
            for copy in moves(i - 1, True):
                copy.wait()
            for copy in moves(i - 1 + depth, False):
                copy.start()

    pl.loop(0, blocks)(advance)

    @pl.loop(max(blocks - depth, 0), blocks)
    def _(i):
        for copy in moves(i, True):
            copy.wait()


def expert_update(rows_x, rows_g, d_pair, acts, weights, moment_one, moment_two):
    replicas, local, slots, part = rows_x.shape
    kinds, ffn = weights.shape[2:]
    block = 32
    twin = min(2, local)
    rows = replicas * slots
    pieces = (rows_x, rows_g, d_pair, acts)
    held = [a.transpose(0, 2, 1, 3) for a in (moment_one, moment_two, weights)]
    depth = 10
    any_spec = pl.BlockSpec(memory_space=pl.ANY)
    out_shape = tuple(jax.ShapeDtypeStruct(a.shape, a.dtype) for a in held)
    kernel = functools.partial(
        update_kernel, (replicas, slots, part, local, kinds, ffn, block, depth)
    )
    outs = pl.pallas_call(
        kernel,
        out_shape=out_shape,
        in_specs=[any_spec] * (len(pieces) + 3),
        out_specs=(any_spec,) * len(out_shape),
        scratch_shapes=[
            pltpu.VMEM((twin, rows, part), BF16),
            pltpu.VMEM((twin, rows, part), BF16),
            pltpu.VMEM((twin, rows, 2 * ffn), BF16),
            pltpu.VMEM((twin, rows, ffn), BF16),
            pltpu.VMEM((kinds * ffn // 128, local * part, 128), F32),
            pltpu.VMEM((depth, block, kinds, local, ffn), F32),
            pltpu.VMEM((depth, block, kinds, local, ffn), F32),
            pltpu.VMEM((depth, block, kinds, local, ffn), BF16),
            pltpu.SemaphoreType.DMA((twin, 4 * replicas)),
            pltpu.SemaphoreType.DMA((3, depth)),
            pltpu.SemaphoreType.DMA((3, depth)),
        ],
        compiler_params=pltpu.CompilerParams(vmem_limit_bytes=60 << 20),
        cost_estimate=pl.CostEstimate(
            flops=2 * rows * part * kinds * ffn * local,
            bytes_accessed=2 * sum(a.size * a.dtype.itemsize for a in held),
            transcendentals=0,
        ),
        name="expert_update",
    )(*pieces, *held)
    return [a.transpose(0, 2, 1, 3) for a in outs]


def forward_kernel(dims, x, g, meta, weights, out_x, out_g, out_pair, out_act, out_home, *scratch):
    replicas, sources, tok, part, local, slots, ffn, cap = dims
    out_dx, scratch = scratch[:sources], scratch[sources:]
    (gx, gg, gm, w, rank, gate, rows_x, rows_g, outgoing, incoming, own, held, raw, turned) = scratch[:14]
    sum_dx, scratch = scratch[14], scratch[15:]
    (own_send, got, sent, w_sem, part_send, part_got, d_send, d_got, out_sem, row_sem) = scratch[:10]
    far_sem, scatter_refs = scratch[10], scratch[11:]
    ring = rows_x.shape[0]
    me, ex = lax.axis_index("rep"), lax.axis_index("exp")
    col, z = ex % 2, ex // 2
    line = sources // 2
    side = ex + 1 - 2 * col
    above, below = z + 1 < line, z >= 1
    pair = 2 * ffn
    order = tuple(reversed(range(replicas)))
    kinds = ((gm, meta), (gx, x), (gg, g))

    barrier = pltpu.get_barrier_semaphore()
    for q in order[:-1]:
        pl.semaphore_signal(barrier, inc=1, device_id={"rep": flip(me, q)}, device_id_type=MESH)
    pl.semaphore_signal(barrier, inc=1, device_id={"exp": side}, device_id_type=MESH)

    @pl.when(above)
    def _():
        pl.semaphore_signal(barrier, inc=1, device_id={"exp": ex + 2}, device_id_type=MESH)

    @pl.when(below)
    def _():
        pl.semaphore_signal(barrier, inc=1, device_id={"exp": ex - 2}, device_id_type=MESH)

    lanes = turned.shape[2]
    chunk = raw.shape[1]
    chunks = part // chunk

    def load_w(c):
        return pltpu.make_async_copy(
            weights.at[pl.ds(c * chunk, chunk)], raw.at[c % 2], w_sem.at[c % 2]
        )

    def turn(c):
        if c + 1 < chunks:
            load_w(c + 1).start()
        load_w(c).wait()
        unroll = 4

        @pl.loop(0, chunk // unroll)
        def _(d4):
            for sub in range(unroll):
                d = d4 * unroll + sub
                for place in range(3 * ffn // lanes):
                    kind, at = divmod(place * lanes, ffn)
                    tile = raw[c % 2, d, kind, :, pl.ds(at, lanes)].astype(F32)
                    turned[place, pl.ds(d, local, stride=chunk), :] = tile

        @pl.loop(0, local)
        def _(l):
            for place in range(3 * ffn // lanes):
                tile = turned[place, pl.ds(pl.multiple_of(l * chunk, chunk), chunk), :]
                w[l, pl.ds(c * chunk, chunk), pl.ds(place * lanes, lanes)] = tile.astype(BF16)

    load_w(0).start()
    expected = replicas + jnp.where(above, 1, 0) + jnp.where(below, 1, 0)
    pl.semaphore_wait(barrier, expected)

    def first(q, n):
        buf, src = kinds[n]
        target = flip(me, q)
        if n:
            src = src.at[:, pl.ds(pl.multiple_of(target * part, part), part)]
        if q == 0:
            return pltpu.make_async_copy(src, buf.at[q, ex], got.at[q, n, ex])
        return pltpu.make_async_remote_copy(
            src_ref=src,
            dst_ref=buf.at[q, ex],
            send_sem=own_send.at[q, n],
            recv_sem=got.at[q, n, ex],
            device_id={"rep": target},
            device_id_type=MESH,
        )

    def hop(q, n, slot, way):
        target = (side, ex + 2, ex - 2)[way]
        return pltpu.make_async_remote_copy(
            src_ref=kinds[n][0].at[q, slot],
            dst_ref=kinds[n][0].at[q, slot],
            send_sem=sent.at[way, q, n, slot],
            recv_sem=got.at[q, n, slot],
            device_id={"exp": target},
            device_id_type=MESH,
        )

    for q in order:
        for n in range(3):
            first(q, n).start()

    def onward(q, n, slot, ways):
        for way in ways:

            @pl.when(above if way == 1 else below)
            def _():
                hop(q, n, slot, way).start()

    def relay_both(q, n, step):
        if step == 0:
            (first(q, n).wait_recv if q else first(q, n).wait)()
            hop(q, n, ex, 0).start()
            onward(q, n, ex, (1, 2))
            return
        if step == 1:
            hop(q, n, side, 0).wait_recv()
            onward(q, n, side, (1, 2))

        @pl.when(z >= step)
        def _():
            for slot in (ex - 2 * step, side - 2 * step):
                hop(q, n, slot, 0).wait_recv()
                onward(q, n, slot, (1,))

        @pl.when(z + step < line)
        def _():
            for slot in (ex + 2 * step, side + 2 * step):
                hop(q, n, slot, 0).wait_recv()
                onward(q, n, slot, (2,))

    def by_both(q, n):
        return line > 1 and (q, n) == (1, 2)

    def relay(q, step, which=(0, 1, 2)):
        for n in which:
            if by_both(q, n):
                relay_both(q, n, step)
                continue
            if step == 0:
                if q:
                    first(q, n).wait_recv()
                else:
                    first(q, n).wait()
                hop(q, n, ex, 0).start()

                @pl.when(above)
                def _():
                    hop(q, n, ex, 1).start()

                @pl.when(below)
                def _():
                    hop(q, n, ex, 2).start()

                continue

            @pl.when(z >= step)
            def _():
                slot = ex - 2 * step
                hop(q, n, slot, 0).wait_recv()
                hop(q, n, slot, 0).start()

                @pl.when(above)
                def _():
                    hop(q, n, slot, 1).start()

            @pl.when(z + step < line)
            def _():
                slot = ex + 2 * step
                hop(q, n, slot, 0).wait_recv()
                hop(q, n, slot, 0).start()

                @pl.when(below)
                def _():
                    hop(q, n, slot, 2).start()

    def settle(q):
        for n in range(3):
            if by_both(q, n):
                continue
            for level in range(line):
                hop(q, n, 2 * level + 1 - col, 0).wait_recv()

    lower = lax.broadcasted_iota(jnp.int32, (tok, tok), 0)
    upper = lax.broadcasted_iota(jnp.int32, (tok, tok), 1)
    earlier = jnp.where(lower < upper, 1.0, 0.0).astype(BF16)
    expert0 = (ex * local).astype(F32)

    def prepare(q):
        @pl.loop(0, sources)
        def _(s):
            info = gm[q, s].astype(F32)[:8]
            routes = info[:, :tok]
            weight = info[:, tok : 2 * tok] + info[:, 2 * tok : 3 * tok] + info[:, 3 * tok :]
            named, gates = [], []
            for l in range(local):
                hit = routes == expert0 + l
                named.append(jnp.max(jnp.where(hit, 1.0, 0.0), axis=0, keepdims=True))
                gates.append(jnp.sum(jnp.where(hit, weight, 0.0), axis=0, keepdims=True))
            named = jnp.concatenate(named, axis=0)
            places = jnp.dot(named.astype(BF16), earlier, preferred_element_type=F32)
            places = jnp.where(named > 0.0, places + (s * cap).astype(F32), -1.0)
            at = pl.ds(pl.multiple_of(s * tok, tok), tok)
            rank[q, :, at] = places
            gate[:, at] = jnp.concatenate(gates, axis=0)

    def exchange(l, q):
        slot, into, bits = {3: (0, 0, 1), 2: (1, 2, 2), 1: (0, 1, 1)}[q]
        return pltpu.make_async_remote_copy(
            src_ref=outgoing.at[slot, l],
            dst_ref=incoming.at[into, l],
            send_sem=part_send.at[q, l],
            recv_sem=part_got.at[into, l],
            device_id={"rep": flip(me, bits)},
            device_id_type=MESH,
        )

    def row_out(l, q):
        slot = (l + (replicas - 1 - q) * local) % ring
        return (
            pltpu.make_async_copy(rows_x.at[slot], out_x.at[q, l], row_sem.at[0, slot]),
            pltpu.make_async_copy(rows_g.at[slot], out_g.at[q, l], row_sem.at[1, slot]),
        )

    def piece(l, q):
        places = rank[q, pl.ds(l, 1), :]
        index = lax.broadcasted_iota(jnp.int32, (slots, sources * tok), 0).astype(F32)
        hit = index == places
        pick = jnp.where(hit, 1.0, 0.0).astype(BF16)
        gates = jnp.sum(jnp.where(hit, gate[pl.ds(l, 1), :], 0.0), axis=1, keepdims=True)
        tokens_x = gx[q].reshape(sources * tok, part)
        tokens_g = gg[q].reshape(sources * tok, part)
        rx = jnp.dot(pick, tokens_x, preferred_element_type=F32).astype(BF16)
        rg = (jnp.dot(pick, tokens_g, preferred_element_type=F32) * gates).astype(BF16)
        turn_of = l + (replicas - 1 - q) * local
        slot = turn_of % ring

        @pl.when(turn_of >= ring)
        def _():
            for copy in row_out(l, q):
                copy.wait()

        rows_x[slot] = rx
        rows_g[slot] = rg
        for copy in row_out(l, q):
            copy.start()
        hidden = jnp.dot(rx, w[l, :, :pair], preferred_element_type=F32)
        da = jnp.dot(rg, w[l, :, pair:], preferred_element_type=F32)
        for lead, width, one in ((0, pair, hidden), (pair, ffn, da)):
            at = pl.ds(lead, width)
            if q == 3:
                outgoing[0, l, :, at] = one.astype(BF16)
            elif q == 2:
                if not lead:
                    exchange(l, 3).wait_recv()
                outgoing[1, l, :, at] = (one + incoming[0, l, :, at].astype(F32)).astype(BF16)
            elif q == 1:
                if not lead:
                    exchange(l, 3).wait_send()
                outgoing[0, l, :, at] = one.astype(BF16)
            else:
                if not lead:
                    exchange(l, 1).wait_recv()
                own[l, :, at] = one + incoming[1, l, :, at].astype(F32)
        if q:
            exchange(l, q).start()

    def grads_to(l, way):
        src, dst, bits = ((0, 1, 1), (0, 2, 2), (2, 3, 1))[way]
        return pltpu.make_async_remote_copy(
            src_ref=held.at[src, l],
            dst_ref=held.at[dst, l],
            send_sem=d_send.at[way, l],
            recv_sem=d_got.at[way, l],
            device_id={"rep": flip(me, bits)},
            device_id_type=MESH,
        )

    def d_out(l, q):
        return (
            pltpu.make_async_copy(
                held.at[q, l, :, pl.ds(0, pair)], out_pair.at[q, l], out_sem.at[0, q, l]
            ),
            pltpu.make_async_copy(
                held.at[q, l, :, pl.ds(pair, ffn)], out_act.at[q, l], out_sem.at[1, q, l]
            ),
        )

    def finish(l):
        exchange(l, 2).wait_recv()
        sums = [
            own[l, :, pl.ds(n * ffn, ffn)] + incoming[2, l, :, pl.ds(n * ffn, ffn)].astype(F32)
            for n in range(3)
        ]
        hg, hu, da = sums
        sig = jax.nn.sigmoid(hg)
        held[0, l, :, pl.ds(2 * ffn, ffn)] = (hg * sig * hu).astype(BF16)
        held[0, l, :, pl.ds(ffn, ffn)] = (da * hg * sig).astype(BF16)
        held[0, l, :, pl.ds(0, ffn)] = (da * hu * sig * (1.0 + hg * (1.0 - sig))).astype(BF16)
        for way in (1, 0):
            grads_to(l, way).start()
        for copy in d_out(l, 0):
            copy.start()

    def pass_on(l):
        grads_to(l, 1).wait_recv()
        grads_to(l, 2).start()
        for copy in d_out(l, 2):
            copy.start()

    def pieces(lo, hi, q):
        @pl.loop(lo, hi)
        def _(l):
            piece(l, q)

    steps = max(line - 1, 1)
    turns = [range(chunks * n // (steps + 1), chunks * (n + 1) // (steps + 1)) for n in range(steps + 1)]
    early = (0, 1)
    for q in early:
        relay(q, 0)
    for c in turns[0]:
        turn(c)
    relay(order[0], 0)
    for i, q in enumerate(order):
        if i + 1 < replicas and order[i + 1] not in early:
            relay(order[i + 1], 0)
        for step in range(1, line):
            for part_of, which in enumerate(((0, 1), (2,))):
                relay(q, step, which)
                n = 2 * (step - 1) + part_of
                if i:
                    pieces(local * n // (2 * steps), local * (n + 1) // (2 * steps), order[i - 1])
                else:
                    mid = (len(turns[step]) + 1) // 2
                    for c in turns[step][mid:] if part_of else turns[step][:mid]:
                        turn(c)
        settle(q)
        prepare(q)

    @pl.loop(0, local)
    def _(l):
        piece(l, order[-1])
        finish(l)

    def sent_blocks(q, n):
        both = by_both(q, n)
        if both:
            hop(q, n, ex, 0).wait_send()

        @pl.loop(0, line)
        def _(level):
            for column in (col, 1 - col) if both else (col,):
                slot = 2 * level + column
                if not both:
                    hop(q, n, slot, 0).wait_send()

                @pl.when(above & (level <= z))
                def _():
                    hop(q, n, slot, 1).wait_send()

                @pl.when(below & (level >= z))
                def _():
                    hop(q, n, slot, 2).wait_send()

    def add_dx(l, q, total):
        hit = lax.broadcasted_iota(jnp.int32, (slots, sources * tok), 0).astype(F32)
        pick = jnp.where(hit == rank[q, pl.ds(l, 1), :], 1.0, 0.0).astype(BF16)
        slot_dx = lax.dot_general(
            held[q, l, :, :pair],
            w[l, :, :pair],
            (((1,), (1,)), ((), ())),
            preferred_element_type=F32,
        ).astype(BF16)
        sum_dx[total] += lax.dot_general(
            pick, slot_dx, (((0,), (0,)), ((), ())), preferred_element_type=F32
        )

    def round_dx(q, total):
        sent_blocks(q, 1)
        gx[q] = sum_dx[total].reshape(sources, tok, part).astype(BF16)

    near = Scatter(
        (0, 1),
        sources,
        lambda j, level: gx.at[j, 2 * level + col],
        lambda j, level: gx.at[j, 2 * level + 1 - col],
        scatter_refs,
    )
    sum_dx[...] = jnp.zeros_like(sum_dx)

    @pl.loop(0, local)
    def _(l):
        add_dx(l, 0, 0)

    round_dx(0, 0)
    near.begin(0)

    @pl.loop(0, local)
    def _(l):
        grads_to(l, 0).wait_recv()
        for copy in d_out(l, 1):
            copy.start()
        add_dx(l, 1, 1)

    round_dx(1, 1)
    near.begin(1)
    sum_dx[...] = jnp.zeros_like(sum_dx)
    for t in range(line - 1):
        for j in range(2):
            near.step(j, t)
    for j in range(2):
        near.finish(j)

    @pl.loop(0, local + 1)
    def _(l):
        @pl.when(l < local)
        def _():
            pass_on(l)
            add_dx(l, 2, 0)

        @pl.when(l >= 1)
        def _():
            grads_to(l - 1, 2).wait_recv()
            for copy in d_out(l - 1, 3):
                copy.start()
            add_dx(l - 1, 3, 1)

    last = []
    for q in (2, 3):
        round_dx(q, q - 2)
        for away in range(sources):
            block = gx.at[q, flip(ex, away)]
            last.append(pltpu.make_async_copy(block, out_dx[away].at[q - 2], far_sem.at[q - 2, away]))
            last[-1].start()
    for j in range(2):
        near.end(j)
    home_copy = pltpu.make_async_copy(near.home, out_home, own_send.at[0, 0])
    home_copy.start()

    @pl.loop(0, local)
    def _(l):
        for q in (2, 1):
            exchange(l, q).wait_send()
        for way in range(3):
            grads_to(l, way).wait_send()
        for q in range(replicas):
            for copy in d_out(l, q):
                copy.wait()

        @pl.when(l >= local - ring)
        def _():
            for copy in row_out(l, 0):
                copy.wait()

    for q in order:
        for n in range(3):
            if q:
                first(q, n).wait_send()
            if n != 1:
                sent_blocks(q, n)
    for copy in (*last, home_copy):
        copy.wait()


def forward(inputs, out_grad, meta, weights, replicas, sources, cap):
    tok = inputs.shape[0]
    part, local, kinds, ffn = weights.shape
    width = kinds * ffn
    chunk = part // 16
    ring = min(4, local)
    slots = sources * cap
    dims = (replicas, sources, tok, part, local, slots, ffn, cap)
    any_spec = pl.BlockSpec(memory_space=pl.ANY)
    rows = (replicas, local, slots)
    dma = pltpu.SemaphoreType.DMA
    return pl.pallas_call(
        functools.partial(forward_kernel, dims),
        out_shape=(
            jax.ShapeDtypeStruct((*rows, part), BF16),
            jax.ShapeDtypeStruct((*rows, part), BF16),
            jax.ShapeDtypeStruct((*rows, 2 * ffn), BF16),
            jax.ShapeDtypeStruct((*rows, ffn), BF16),
            *[jax.ShapeDtypeStruct((2, tok, part), BF16)] * (1 + sources),
        ),
        in_specs=[any_spec] * 4,
        out_specs=(any_spec,) * (5 + sources),
        scratch_shapes=[
            pltpu.VMEM((replicas, sources, tok, part), BF16),
            pltpu.VMEM((replicas, sources, tok, part), BF16),
            pltpu.VMEM((replicas, sources, *meta.shape), BF16),
            pltpu.VMEM((local, part, width), BF16),
            pltpu.VMEM((replicas, local, sources * tok), F32),
            pltpu.VMEM((local, sources * tok), F32),
            pltpu.VMEM((ring, slots, part), BF16),
            pltpu.VMEM((ring, slots, part), BF16),
            pltpu.VMEM((2, local, slots, width), BF16),
            pltpu.VMEM((3, local, slots, width), BF16),
            pltpu.VMEM((local, slots, width), F32),
            pltpu.VMEM((*rows, width), BF16),
            pltpu.VMEM((2, chunk, kinds, local, ffn), BF16),
            pltpu.VMEM((width // 128, local * chunk, 128), F32),
            pltpu.VMEM((2, sources * tok, part), F32),
            dma((replicas, 3)),
            dma((replicas, 3, sources)),
            dma((3, replicas, 3, sources)),
            dma((2,)),
            dma((replicas, local)),
            dma((3, local)),
            dma((3, local)),
            dma((3, local)),
            dma((2, replicas, local)),
            dma((2, ring)),
            dma((2, sources)),
            *scatter_scratch(2, sources, tok, part),
        ],
        compiler_params=pltpu.CompilerParams(
            collective_id=0, has_side_effects=True, vmem_limit_bytes=63 << 20
        ),
        name="gather_forward",
    )(inputs, out_grad, meta, weights.transpose(0, 2, 1, 3))


def by_collectives(inputs, out_grad, terms, weights, top, sources, swap):
    replicas = lax.axis_size("rep")
    me = lax.axis_index("rep")
    tok_dev = inputs.shape[0]
    part, local, kinds, ffn = weights.shape
    pair = 2 * ffn
    slots = sources * CAP
    half = max(replicas // 2, 1)
    mats = weights.transpose(1, 0, 2, 3).reshape(local, part, kinds * ffn)
    meta = jnp.concatenate(terms).reshape(-1, part)
    meta_rows = meta.shape[0]
    pad = -meta_rows % 16
    meta = jnp.pad(meta, ((0, pad), (0, 0)))

    def arrive(q):
        at = (me ^ q) * part
        x = lax.dynamic_slice_in_dim(inputs, at, part, 1)
        g = lax.dynamic_slice_in_dim(out_grad, at, part, 1)
        return swap(jnp.concatenate([x, g, meta]), q)

    gathered = {}
    for start in range(replicas - half, -1, -half):
        chosen = range(start, start + half)
        block = jnp.stack([arrive(q) for q in reversed(chosen)])
        block = lax.all_gather(block, "exp", axis=0, tiled=False)
        for place, q in enumerate(reversed(chosen)):
            gathered[q] = block[:, place]

    mine = lax.axis_index("exp") * local + jnp.arange(local, dtype=jnp.int32)
    earlier = jnp.arange(tok_dev)[:, None] < jnp.arange(tok_dev)[None, :]
    base = (jnp.arange(sources) * CAP).astype(F32)
    pair_mats, down_mats = mats[..., :pair], mats[..., pair:]
    picks, rows_x, rows_g, arrivals = {}, {}, {}, {}
    for q in reversed(range(replicas)):
        if q == half - 1 and replicas > 1:
            later = {p: gathered[p] for p in range(half)}
            later, _ = lax.optimization_barrier((later, sent))
            gathered.update(later)
        got = gathered[q]
        info = got[:, 2 * tok_dev : 2 * tok_dev + meta_rows].astype(F32)
        info = info.reshape(sources, 4, top, tok_dev)
        weight = info[:, 1] + info[:, 2] + info[:, 3]
        hit = info[:, 0][None] == mine.astype(F32)[:, None, None, None]
        named = jnp.any(hit, axis=2)
        gate = jnp.sum(jnp.where(hit, weight[None], 0.0), axis=2)
        rank = jnp.einsum(
            "let,tu->leu", named.astype(BF16), earlier.astype(BF16), preferred_element_type=F32
        )
        rank = jnp.where(named, rank + base[None, :, None], -1.0)
        rank = rank.reshape(local, 1, sources * tok_dev)
        onehot = rank == jnp.arange(slots, dtype=F32)[None, :, None]
        gate = gate.reshape(local, 1, sources * tok_dev)
        gate_slot = jnp.sum(jnp.where(onehot, gate, 0.0), axis=2)
        picks[q] = onehot.astype(BF16)
        tokens_x = got[:, :tok_dev].reshape(sources * tok_dev, part)
        tokens_g = got[:, tok_dev : 2 * tok_dev].reshape(sources * tok_dev, part)
        x = jnp.einsum("lst,td->lsd", picks[q], tokens_x, preferred_element_type=F32)
        g = jnp.einsum("lst,td->lsd", picks[q], tokens_g, preferred_element_type=F32)
        rows_x[q] = x.astype(BF16)
        rows_g[q] = (g * gate_slot[..., None]).astype(BF16)
        hidden = jnp.einsum("lrd,ldh->lrh", rows_x[q], pair_mats, preferred_element_type=F32)
        da = jnp.einsum("lrd,ldh->lrh", rows_g[q], down_mats, preferred_element_type=F32)
        sums = [hidden, da]
        for term in arrivals.pop(q, []):
            sums = [old + new.astype(F32) for old, new in zip(sums, term)]
        sent = [one.astype(BF16) for one in sums]
        if q:
            arrivals.setdefault(q & (q - 1), []).append([swap(one, q & -q) for one in sent])

    hidden, da = sums
    hg, hu = hidden[..., :ffn], hidden[..., ffn:]
    sig = jax.nn.sigmoid(hg)
    act = (hg * sig * hu).astype(BF16)
    dhu = (da * hg * sig).astype(BF16)
    dhg = (da * hu * sig * (1.0 + hg * (1.0 - sig))).astype(BF16)
    d_pair, acts = {0: jnp.concatenate([dhg, dhu], axis=2)}, {0: act}
    for held in (d_pair, acts):
        bit = replicas // 2
        while bit:
            for q in list(held):
                held[q ^ bit] = swap(held[q], bit)
            bit //= 2

    token_dx = {}
    for q in range(replicas):
        slot_dx = jnp.einsum(
            "lrh,ldh->lrd", d_pair[q], pair_mats, preferred_element_type=F32
        ).astype(BF16)
        dx = jnp.einsum("lst,lsd->td", picks[q], slot_dx, preferred_element_type=F32)
        token_dx[q] = dx.astype(BF16).reshape(sources, tok_dev, part)
    home = {}
    for start in range(0, replicas, half):
        block = jnp.concatenate([token_dx[q] for q in range(start, start + half)], axis=1)
        block = lax.psum_scatter(block, "exp", scatter_dimension=0, tiled=False)
        for place in range(half):
            one = block[place * tok_dev : (place + 1) * tok_dev]
            home[start + place] = swap(one, start + place)
    home = jnp.stack([home[q] for q in range(replicas)])

    def stacked(pieces):
        return jnp.stack([pieces[q] for q in range(replicas)])

    return stacked(rows_x), stacked(rows_g), stacked(d_pair), stacked(acts), home


def per_device(inputs, out_grad, routes, gates, weights, moment_one, moment_two):
    replicas, sources = lax.axis_size("rep"), lax.axis_size("exp")
    tok_dev, top = routes.shape
    part, local, kinds, ffn = weights.shape
    slots = sources * CAP
    me = lax.axis_index("rep")

    def swap(array, bits):
        if bits == 0:
            return array
        return lax.ppermute(array, "rep", [(i, i ^ bits) for i in range(replicas)])

    terms, rest = [routes.astype(BF16).T], gates.T
    for _ in range(3):
        head = lax.reduce_precision(rest, 8, 7)
        terms.append(head.astype(BF16))
        rest = rest - head
    at_once = 2 * replicas * sources * tok_dev * part + 20 * local * slots * kinds * ffn
    if replicas == 4 and sources >= 2 and sources & (sources - 1) == 0 and at_once < 32 << 20:
        meta = jnp.concatenate(terms, axis=1)
        meta = jnp.pad(meta, ((0, -top % 16), (0, 0)))
        *grown, near, own_dx = (outs := forward(
            inputs, out_grad, meta, weights, replicas, sources, CAP
        ))[:6]
        came = []
        for away, block in enumerate(outs[6:], 1):
            pairs = [(i, i ^ away) for i in range(sources)]
            came.append(lax.ppermute(block, "exp", pairs))
        first_moment, second_moment, new_weights = expert_update(
            *grown, weights, moment_one, moment_two
        )
        far = sum([block.astype(F32) for block in came], own_dx.astype(F32)).astype(BF16)
        far = [swap(far[j], j + 2) for j in range(2)]
        home = jnp.concatenate([near, jnp.stack(far)])
    else:
        *grown, home = by_collectives(inputs, out_grad, terms, weights, top, sources, swap)
        first_moment, second_moment, new_weights = expert_update(
            *grown, weights, moment_one, moment_two
        )
    input_grad = jnp.concatenate(
        [lax.dynamic_index_in_dim(home, me ^ q, 0, keepdims=False) for q in range(replicas)],
        axis=1,
    )
    return (input_grad, first_moment, second_moment, new_weights)


def solution(mesh):
    tokens = P(("rep", "exp"), None)
    experts = P("rep", "exp", None, None)
    return jax.shard_map(
        per_device,
        mesh=mesh,
        in_specs=(tokens, tokens, tokens, tokens, experts, experts, experts),
        out_specs=(tokens, experts, experts, experts),
        check_vma=False,
    )
```

```python
import functools

import jax
import jax.numpy as jnp
from jax import lax
from jax.experimental import pallas as pl
from jax.experimental.pallas import tpu as pltpu
from jax.sharding import PartitionSpec as P


CAP = 18


beta_one = 0.9
beta_two = 0.95
learn_rate = 0.002
decay_rate = 0.1
epsilon = 1e-08
step_count = 100

F32 = jnp.float32
BF16 = jnp.bfloat16


MESH = pl.DeviceIdType.MESH


def flip(index, bits):
    for place in range(bits.bit_length()):
        bit = 1 << place
        if bits & bit:
            index = index + bit * (1 - 2 * ((index // bit) % 2))
    return index


class Scatter:
    def __init__(self, parts, sources, mine, theirs, refs):
        self.parts, self.mine, self.theirs = parts, mine, theirs
        self.from_side, self.from_z, self.total, self.home = refs[:4]
        self.y_send, self.y_got, self.z_send, self.z_got, self.h_send, self.h_got = refs[4:]
        self.me, self.ex = lax.axis_index("rep"), lax.axis_index("exp")
        self.col, self.z, self.line = self.ex % 2, self.ex // 2, sources // 2
        self.side = self.ex + 1 - 2 * self.col
        self.above, self.below = self.z + 1 < self.line, self.z >= 1

    def across(self, j, level):
        return pltpu.make_async_remote_copy(
            src_ref=self.theirs(j, level),
            dst_ref=self.from_side.at[j, level],
            send_sem=self.y_send.at[j, level],
            recv_sem=self.y_got.at[j, level],
            device_id={"exp": self.side},
            device_id_type=MESH,
        )

    def along(self, j, level, way):
        return pltpu.make_async_remote_copy(
            src_ref=self.mine(j, level),
            dst_ref=self.from_z.at[way, j, level],
            send_sem=self.z_send.at[way, j, level],
            recv_sem=self.z_got.at[way, j, level],
            device_id={"exp": self.ex + (2 if way == 0 else -2)},
            device_id_type=MESH,
        )

    def homeward(self, j):
        q = self.parts[j]
        if q == 0:
            return pltpu.make_async_copy(self.total.at[j], self.home.at[j], self.h_got.at[j])
        return pltpu.make_async_remote_copy(
            src_ref=self.total.at[j],
            dst_ref=self.home.at[j],
            send_sem=self.h_send.at[j],
            recv_sem=self.h_got.at[j],
            device_id={"rep": flip(self.me, q)},
            device_id_type=MESH,
        )

    def begin(self, j):
        for t in range((self.line + 1) // 2):
            for level in sorted({self.line - 1 - t, t}, reverse=True):
                self.across(j, level).start()

    def add(self, j, level, ways, into):
        into[...] = sum(
            [self.from_z[way, j, level].astype(F32) for way in ways],
            self.mine(j, level)[...].astype(F32) + self.from_side[j, level].astype(F32),
        ).astype(BF16)

    def step(self, j, t):
        for way, level, near, fed in (
            (0, self.line - 1 - t, self.z < self.line - 1 - t, self.below),
            (1, t, self.z > t, self.above),
        ):

            @pl.when(near)
            def _():
                self.across(j, level).wait_recv()

                @pl.when(fed)
                def _():
                    self.along(j, level, way).wait_recv()
                    self.add(j, level, (way,), self.mine(j, level))

                @pl.when(jnp.logical_not(fed))
                def _():
                    self.add(j, level, (), self.mine(j, level))

                self.along(j, level, way).start()

    def finish(self, j):
        for level in range(self.line):

            @pl.when(self.z == level)
            def _():
                self.across(j, level).wait_recv()
                ways = [0] * (level >= 1) + [1] * (level + 1 < self.line)
                for way in ways:
                    self.along(j, level, way).wait_recv()
                self.add(j, level, ways, self.total.at[j])

        self.homeward(j).start()

    def end(self, j):
        if self.parts[j]:
            self.homeward(j).wait_recv()
            self.homeward(j).wait_send()
        else:
            self.homeward(j).wait()
        for level in range(self.line):
            self.across(j, level).wait_send()

            @pl.when(self.z < level)
            def _():
                self.along(j, level, 0).wait_send()

            @pl.when(self.z > level)
            def _():
                self.along(j, level, 1).wait_send()


def scatter_scratch(parts, sources, tok, part):
    line = sources // 2
    dma = pltpu.SemaphoreType.DMA
    return [
        pltpu.VMEM((parts, line, tok, part), BF16),
        pltpu.VMEM((2, parts, line, tok, part), BF16),
        pltpu.VMEM((parts, tok, part), BF16),
        pltpu.VMEM((parts, tok, part), BF16),
        dma((parts, line)),
        dma((parts, line)),
        dma((2, parts, line)),
        dma((2, parts, line)),
        dma((parts,)),
        dma((parts,)),
    ]


def update_kernel(dims, *refs):
    (replicas, slots, part, local, kinds, ffn, block, depth) = dims
    pieces, refs = refs[:4], refs[4:]
    m_one, m_two, w_in, o_one, o_two, w_out = refs[:6]
    bufs, (grad, b_one, b_two, b_w, in_sem, load_sem, store_sem) = refs[6:10], refs[10:]
    rows = replicas * slots
    twin = min(2, local)
    blocks = part // block
    ahead = min(depth, blocks)
    lanes = grad.shape[2]

    def fetch(e, go):
        for kind in range(4):
            for q in range(replicas):
                n = kind * replicas + q
                copy = pltpu.make_async_copy(
                    pieces[kind].at[q, e],
                    bufs[kind].at[lax.rem(e, twin), pl.ds(q * slots, slots)],
                    in_sem.at[lax.rem(e, twin), n],
                )
                copy.start() if go else copy.wait()

    def moves(i, outward):
        s = lax.rem(i, depth)
        part_of = pl.ds(i * block, block)
        if outward:
            trio = ((b_one, o_one), (b_two, o_two), (b_w, w_out))
            return [
                pltpu.make_async_copy(a.at[s], b.at[part_of], store_sem.at[n, s])
                for n, (a, b) in enumerate(trio)
            ]
        trio = ((b_one, m_one), (b_two, m_two), (b_w, w_in))
        return [
            pltpu.make_async_copy(b.at[part_of], a.at[s], load_sem.at[n, s])
            for n, (a, b) in enumerate(trio)
        ]

    fetch(0, True)

    @pl.loop(0, ahead)
    def _(i):
        for copy in moves(i, False):
            copy.start()

    @pl.loop(0, local)
    def _(e):
        if twin > 1:

            @pl.when(e + 1 < local)
            def _():
                fetch(e + 1, True)

        fetch(e, False)
        at = lax.rem(e, twin)
        base = pl.multiple_of(e * part, part)
        step = rows if rows <= 1024 else slots
        for lead, width, left, right in ((0, 2 * ffn, 0, 2), (2 * ffn, ffn, 1, 3)):
            for start in range(0, rows, step):
                one = lax.dot_general(
                    bufs[left][at, pl.ds(start, step), :],
                    bufs[right][at, pl.ds(start, step), :],
                    (((0,), (0,)), ((), ())),
                    preferred_element_type=F32,
                )
                for c in range(width // lanes):
                    tile = one[:, c * lanes : (c + 1) * lanes]
                    place = lead // lanes + c
                    if start:
                        tile = tile + grad[place, pl.ds(base, part), :]
                    grad[place, pl.ds(base, part), :] = tile

    correct_one = 1.0 - beta_one**step_count
    correct_two = 1.0 - beta_two**step_count

    def advance(i):
        s = lax.rem(i, depth)
        for copy in moves(i, False):
            copy.wait()

        @pl.loop(0, block // 4)
        def _(pair):
            spots = []
            for sub in range(4):
                row = pair * 4 + sub
                d = i * block + row
                of_d = pl.ds(d, local, stride=part) if local > 1 else pl.ds(d, 1)
                for place in range(kinds * ffn // lanes):
                    kind, c = divmod(place * lanes, ffn)
                    spots.append(((s, row, kind, slice(None), pl.ds(c, lanes)), place, of_d))
            held = [(b_one[at], b_two[at], b_w[at], grad[place, of_d, :]) for at, place, of_d in spots]
            done = []
            for one, two, w, g in held:
                first = beta_one * one + (1.0 - beta_one) * g
                second = beta_two * two + (1.0 - beta_two) * g * g
                w = w.astype(F32)
                root = jnp.sqrt(second * (1.0 / correct_two)) + epsilon
                update = first * (1.0 / correct_one) / root + decay_rate * w
                done.append((first, second, (w - learn_rate * update).astype(BF16)))
            for (at, _, _), (first, second, new) in zip(spots, done):
                b_one[at] = first
                b_two[at] = second
                b_w[at] = new

        for copy in moves(i, True):
            copy.start()

        @pl.when((i >= 1) & (i - 1 + depth < blocks))
        def _():
            for copy in moves(i - 1, True):
                copy.wait()
            for copy in moves(i - 1 + depth, False):
                copy.start()

    pl.loop(0, blocks)(advance)

    @pl.loop(max(blocks - depth, 0), blocks)
    def _(i):
        for copy in moves(i, True):
            copy.wait()


def expert_update(rows_x, rows_g, d_pair, acts, weights, moment_one, moment_two):
    replicas, local, slots, part = rows_x.shape
    kinds, ffn = weights.shape[2:]
    block = 32
    twin = min(2, local)
    rows = replicas * slots
    pieces = (rows_x, rows_g, d_pair, acts)
    held = [a.transpose(0, 2, 1, 3) for a in (moment_one, moment_two, weights)]
    depth = 10
    any_spec = pl.BlockSpec(memory_space=pl.ANY)
    out_shape = tuple(jax.ShapeDtypeStruct(a.shape, a.dtype) for a in held)
    kernel = functools.partial(
        update_kernel, (replicas, slots, part, local, kinds, ffn, block, depth)
    )
    outs = pl.pallas_call(
        kernel,
        out_shape=out_shape,
        in_specs=[any_spec] * (len(pieces) + 3),
        out_specs=(any_spec,) * len(out_shape),
        scratch_shapes=[
            pltpu.VMEM((twin, rows, part), BF16),
            pltpu.VMEM((twin, rows, part), BF16),
            pltpu.VMEM((twin, rows, 2 * ffn), BF16),
            pltpu.VMEM((twin, rows, ffn), BF16),
            pltpu.VMEM((kinds * ffn // 128, local * part, 128), F32),
            pltpu.VMEM((depth, block, kinds, local, ffn), F32),
            pltpu.VMEM((depth, block, kinds, local, ffn), F32),
            pltpu.VMEM((depth, block, kinds, local, ffn), BF16),
            pltpu.SemaphoreType.DMA((twin, 4 * replicas)),
            pltpu.SemaphoreType.DMA((3, depth)),
            pltpu.SemaphoreType.DMA((3, depth)),
        ],
        compiler_params=pltpu.CompilerParams(vmem_limit_bytes=60 << 20),
        cost_estimate=pl.CostEstimate(
            flops=2 * rows * part * kinds * ffn * local,
            bytes_accessed=2 * sum(a.size * a.dtype.itemsize for a in held),
            transcendentals=0,
        ),
        name="expert_update",
    )(*pieces, *held)
    return [a.transpose(0, 2, 1, 3) for a in outs]


def forward_kernel(dims, x, g, meta, weights, out_x, out_g, out_pair, out_act, out_home, *scratch):
    replicas, sources, tok, part, local, slots, ffn, cap = dims
    out_dx, scratch = scratch[:sources], scratch[sources:]
    (gx, gg, gm, w, rank, gate, rows_x, rows_g, outgoing, incoming, own, held, raw, turned) = scratch[:14]
    sum_dx, scratch = scratch[14], scratch[15:]
    (own_send, got, sent, w_sem, part_send, part_got, d_send, d_got, out_sem, row_sem) = scratch[:10]
    far_sem, scatter_refs = scratch[10], scratch[11:]
    ring = rows_x.shape[0]
    me, ex = lax.axis_index("rep"), lax.axis_index("exp")
    col, z = ex % 2, ex // 2
    line = sources // 2
    side = ex + 1 - 2 * col
    above, below = z + 1 < line, z >= 1
    pair = 2 * ffn
    order = tuple(reversed(range(replicas)))
    kinds = ((gm, meta), (gx, x), (gg, g))

    barrier = pltpu.get_barrier_semaphore()
    for q in order[:-1]:
        pl.semaphore_signal(barrier, inc=1, device_id={"rep": flip(me, q)}, device_id_type=MESH)
    pl.semaphore_signal(barrier, inc=1, device_id={"exp": side}, device_id_type=MESH)

    @pl.when(above)
    def _():
        pl.semaphore_signal(barrier, inc=1, device_id={"exp": ex + 2}, device_id_type=MESH)

    @pl.when(below)
    def _():
        pl.semaphore_signal(barrier, inc=1, device_id={"exp": ex - 2}, device_id_type=MESH)

    lanes = turned.shape[2]
    chunk = raw.shape[1]
    chunks = part // chunk

    def load_w(c):
        return pltpu.make_async_copy(
            weights.at[pl.ds(c * chunk, chunk)], raw.at[c % 2], w_sem.at[c % 2]
        )

    def turn(c):
        if c + 1 < chunks:
            load_w(c + 1).start()
        load_w(c).wait()
        unroll = 4

        @pl.loop(0, chunk // unroll)
        def _(d4):
            for sub in range(unroll):
                d = d4 * unroll + sub
                for place in range(3 * ffn // lanes):
                    kind, at = divmod(place * lanes, ffn)
                    tile = raw[c % 2, d, kind, :, pl.ds(at, lanes)].astype(F32)
                    turned[place, pl.ds(d, local, stride=chunk), :] = tile

        @pl.loop(0, local)
        def _(l):
            for place in range(3 * ffn // lanes):
                tile = turned[place, pl.ds(pl.multiple_of(l * chunk, chunk), chunk), :]
                w[l, pl.ds(c * chunk, chunk), pl.ds(place * lanes, lanes)] = tile.astype(BF16)

    load_w(0).start()
    expected = replicas + jnp.where(above, 1, 0) + jnp.where(below, 1, 0)
    pl.semaphore_wait(barrier, expected)

    def first(q, n):
        buf, src = kinds[n]
        target = flip(me, q)
        if n:
            src = src.at[:, pl.ds(pl.multiple_of(target * part, part), part)]
        if q == 0:
            return pltpu.make_async_copy(src, buf.at[q, ex], got.at[q, n, ex])
        return pltpu.make_async_remote_copy(
            src_ref=src,
            dst_ref=buf.at[q, ex],
            send_sem=own_send.at[q, n],
            recv_sem=got.at[q, n, ex],
            device_id={"rep": target},
            device_id_type=MESH,
        )

    def hop(q, n, slot, way):
        target = (side, ex + 2, ex - 2)[way]
        return pltpu.make_async_remote_copy(
            src_ref=kinds[n][0].at[q, slot],
            dst_ref=kinds[n][0].at[q, slot],
            send_sem=sent.at[way, q, n, slot],
            recv_sem=got.at[q, n, slot],
            device_id={"exp": target},
            device_id_type=MESH,
        )

    for q in order:
        for n in range(3):
            first(q, n).start()

    def onward(q, n, slot, ways):
        for way in ways:

            @pl.when(above if way == 1 else below)
            def _():
                hop(q, n, slot, way).start()

    def relay_both(q, n, step):
        if step == 0:
            (first(q, n).wait_recv if q else first(q, n).wait)()
            hop(q, n, ex, 0).start()
            onward(q, n, ex, (1, 2))
            return
        if step == 1:
            hop(q, n, side, 0).wait_recv()
            onward(q, n, side, (1, 2))

        @pl.when(z >= step)
        def _():
            for slot in (ex - 2 * step, side - 2 * step):
                hop(q, n, slot, 0).wait_recv()
                onward(q, n, slot, (1,))

        @pl.when(z + step < line)
        def _():
            for slot in (ex + 2 * step, side + 2 * step):
                hop(q, n, slot, 0).wait_recv()
                onward(q, n, slot, (2,))

    def by_both(q, n):
        return line > 1 and (q, n) == (1, 2)

    def relay(q, step, which=(0, 1, 2)):
        for n in which:
            if by_both(q, n):
                relay_both(q, n, step)
                continue
            if step == 0:
                if q:
                    first(q, n).wait_recv()
                else:
                    first(q, n).wait()
                hop(q, n, ex, 0).start()

                @pl.when(above)
                def _():
                    hop(q, n, ex, 1).start()

                @pl.when(below)
                def _():
                    hop(q, n, ex, 2).start()

                continue

            @pl.when(z >= step)
            def _():
                slot = ex - 2 * step
                hop(q, n, slot, 0).wait_recv()
                hop(q, n, slot, 0).start()

                @pl.when(above)
                def _():
                    hop(q, n, slot, 1).start()

            @pl.when(z + step < line)
            def _():
                slot = ex + 2 * step
                hop(q, n, slot, 0).wait_recv()
                hop(q, n, slot, 0).start()

                @pl.when(below)
                def _():
                    hop(q, n, slot, 2).start()

    def settle(q):
        for n in range(3):
            if by_both(q, n):
                continue
            for level in range(line):
                hop(q, n, 2 * level + 1 - col, 0).wait_recv()

    lower = lax.broadcasted_iota(jnp.int32, (tok, tok), 0)
    upper = lax.broadcasted_iota(jnp.int32, (tok, tok), 1)
    earlier = jnp.where(lower < upper, 1.0, 0.0).astype(BF16)
    expert0 = (ex * local).astype(F32)

    def prepare(q):
        @pl.loop(0, sources)
        def _(s):
            info = gm[q, s].astype(F32)[:8]
            routes = info[:, :tok]
            weight = info[:, tok : 2 * tok] + info[:, 2 * tok : 3 * tok] + info[:, 3 * tok :]
            named, gates = [], []
            for l in range(local):
                hit = routes == expert0 + l
                named.append(jnp.max(jnp.where(hit, 1.0, 0.0), axis=0, keepdims=True))
                gates.append(jnp.sum(jnp.where(hit, weight, 0.0), axis=0, keepdims=True))
            named = jnp.concatenate(named, axis=0)
            places = jnp.dot(named.astype(BF16), earlier, preferred_element_type=F32)
            places = jnp.where(named > 0.0, places + (s * cap).astype(F32), -1.0)
            at = pl.ds(pl.multiple_of(s * tok, tok), tok)
            rank[q, :, at] = places
            gate[:, at] = jnp.concatenate(gates, axis=0)

    def exchange(l, q):
        slot, into, bits = {3: (0, 0, 1), 2: (1, 2, 2), 1: (0, 1, 1)}[q]
        return pltpu.make_async_remote_copy(
            src_ref=outgoing.at[slot, l],
            dst_ref=incoming.at[into, l],
            send_sem=part_send.at[q, l],
            recv_sem=part_got.at[into, l],
            device_id={"rep": flip(me, bits)},
            device_id_type=MESH,
        )

    def row_out(l, q):
        slot = (l + (replicas - 1 - q) * local) % ring
        return (
            pltpu.make_async_copy(rows_x.at[slot], out_x.at[q, l], row_sem.at[0, slot]),
            pltpu.make_async_copy(rows_g.at[slot], out_g.at[q, l], row_sem.at[1, slot]),
        )

    def piece(l, q):
        places = rank[q, pl.ds(l, 1), :]
        index = lax.broadcasted_iota(jnp.int32, (slots, sources * tok), 0).astype(F32)
        hit = index == places
        pick = jnp.where(hit, 1.0, 0.0).astype(BF16)
        gates = jnp.sum(jnp.where(hit, gate[pl.ds(l, 1), :], 0.0), axis=1, keepdims=True)
        tokens_x = gx[q].reshape(sources * tok, part)
        tokens_g = gg[q].reshape(sources * tok, part)
        rx = jnp.dot(pick, tokens_x, preferred_element_type=F32).astype(BF16)
        rg = (jnp.dot(pick, tokens_g, preferred_element_type=F32) * gates).astype(BF16)
        turn_of = l + (replicas - 1 - q) * local
        slot = turn_of % ring

        @pl.when(turn_of >= ring)
        def _():
            for copy in row_out(l, q):
                copy.wait()

        rows_x[slot] = rx
        rows_g[slot] = rg
        for copy in row_out(l, q):
            copy.start()
        hidden = jnp.dot(rx, w[l, :, :pair], preferred_element_type=F32)
        da = jnp.dot(rg, w[l, :, pair:], preferred_element_type=F32)
        for lead, width, one in ((0, pair, hidden), (pair, ffn, da)):
            at = pl.ds(lead, width)
            if q == 3:
                outgoing[0, l, :, at] = one.astype(BF16)
            elif q == 2:
                if not lead:
                    exchange(l, 3).wait_recv()
                outgoing[1, l, :, at] = (one + incoming[0, l, :, at].astype(F32)).astype(BF16)
            elif q == 1:
                if not lead:
                    exchange(l, 3).wait_send()
                outgoing[0, l, :, at] = one.astype(BF16)
            else:
                if not lead:
                    exchange(l, 1).wait_recv()
                own[l, :, at] = one + incoming[1, l, :, at].astype(F32)
        if q:
            exchange(l, q).start()

    def grads_to(l, way):
        src, dst, bits = ((0, 1, 1), (0, 2, 2), (2, 3, 1))[way]
        return pltpu.make_async_remote_copy(
            src_ref=held.at[src, l],
            dst_ref=held.at[dst, l],
            send_sem=d_send.at[way, l],
            recv_sem=d_got.at[way, l],
            device_id={"rep": flip(me, bits)},
            device_id_type=MESH,
        )

    def d_out(l, q):
        return (
            pltpu.make_async_copy(
                held.at[q, l, :, pl.ds(0, pair)], out_pair.at[q, l], out_sem.at[0, q, l]
            ),
            pltpu.make_async_copy(
                held.at[q, l, :, pl.ds(pair, ffn)], out_act.at[q, l], out_sem.at[1, q, l]
            ),
        )

    def finish(l):
        exchange(l, 2).wait_recv()
        sums = [
            own[l, :, pl.ds(n * ffn, ffn)] + incoming[2, l, :, pl.ds(n * ffn, ffn)].astype(F32)
            for n in range(3)
        ]
        hg, hu, da = sums
        sig = jax.nn.sigmoid(hg)
        held[0, l, :, pl.ds(2 * ffn, ffn)] = (hg * sig * hu).astype(BF16)
        held[0, l, :, pl.ds(ffn, ffn)] = (da * hg * sig).astype(BF16)
        held[0, l, :, pl.ds(0, ffn)] = (da * hu * sig * (1.0 + hg * (1.0 - sig))).astype(BF16)
        for way in (1, 0):
            grads_to(l, way).start()
        for copy in d_out(l, 0):
            copy.start()

    def pass_on(l):
        grads_to(l, 1).wait_recv()
        grads_to(l, 2).start()
        for copy in d_out(l, 2):
            copy.start()

    def pieces(lo, hi, q):
        @pl.loop(lo, hi)
        def _(l):
            piece(l, q)

    steps = max(line - 1, 1)
    turns = [range(chunks * n // (steps + 1), chunks * (n + 1) // (steps + 1)) for n in range(steps + 1)]
    early = (0, 1)
    for q in early:
        relay(q, 0)
    for c in turns[0]:
        turn(c)
    relay(order[0], 0)
    for i, q in enumerate(order):
        if i + 1 < replicas and order[i + 1] not in early:
            relay(order[i + 1], 0)
        for step in range(1, line):
            for part_of, which in enumerate(((0, 1), (2,))):
                relay(q, step, which)
                n = 2 * (step - 1) + part_of
                if i:
                    pieces(local * n // (2 * steps), local * (n + 1) // (2 * steps), order[i - 1])
                else:
                    mid = (len(turns[step]) + 1) // 2
                    for c in turns[step][mid:] if part_of else turns[step][:mid]:
                        turn(c)
        settle(q)
        prepare(q)

    @pl.loop(0, local)
    def _(l):
        piece(l, order[-1])
        finish(l)

    def sent_blocks(q, n):
        both = by_both(q, n)
        if both:
            hop(q, n, ex, 0).wait_send()

        @pl.loop(0, line)
        def _(level):
            for column in (col, 1 - col) if both else (col,):
                slot = 2 * level + column
                if not both:
                    hop(q, n, slot, 0).wait_send()

                @pl.when(above & (level <= z))
                def _():
                    hop(q, n, slot, 1).wait_send()

                @pl.when(below & (level >= z))
                def _():
                    hop(q, n, slot, 2).wait_send()

    def add_dx(l, q, total, count):
        index = lax.broadcasted_iota(jnp.int32, (slots, sources * tok), 0).astype(F32)
        picks, terms = [], []
        for more in range(count):
            hit = index == rank[q, pl.ds(l + more, 1), :]
            picks.append(jnp.where(hit, 1.0, 0.0).astype(BF16))
            slot_dx = lax.dot_general(
                held[q, l + more, :, :pair],
                w[l + more, :, :pair],
                (((1,), (1,)), ((), ())),
                preferred_element_type=F32,
            )
            terms.append(slot_dx.astype(BF16))
        sum_dx[total] += lax.dot_general(
            jnp.concatenate(picks, axis=0),
            jnp.concatenate(terms, axis=0),
            (((0,), (0,)), ((), ())),
            preferred_element_type=F32,
        )

    few = 2 if local % 2 == 0 else 1
    many = 4 if local % 4 == 0 else few

    def round_dx(q, total):
        sent_blocks(q, 1)
        gx[q] = sum_dx[total].reshape(sources, tok, part).astype(BF16)

    near = Scatter(
        (0, 1),
        sources,
        lambda j, level: gx.at[j, 2 * level + col],
        lambda j, level: gx.at[j, 2 * level + 1 - col],
        scatter_refs,
    )
    sum_dx[...] = jnp.zeros_like(sum_dx)

    @pl.loop(0, local // many)
    def _(n):
        add_dx(n * many, 0, 0, many)

    round_dx(0, 0)
    near.begin(0)

    @pl.loop(0, local)
    def _(l):
        grads_to(l, 0).wait_recv()
        for copy in d_out(l, 1):
            copy.start()

    @pl.loop(0, local // many)
    def _(n):
        add_dx(n * many, 1, 1, many)

    round_dx(1, 1)
    near.begin(1)
    sum_dx[...] = jnp.zeros_like(sum_dx)
    for t in range(line - 1):
        for j in range(2):
            near.step(j, t)
    for j in range(2):
        near.finish(j)

    @pl.loop(0, local // few + 1)
    def _(n):
        @pl.when(n < local // few)
        def _():
            for more in range(few):
                pass_on(n * few + more)
            add_dx(n * few, 2, 0, few)

        @pl.when(n >= 1)
        def _():
            for more in range(few):
                l = (n - 1) * few + more
                grads_to(l, 2).wait_recv()
                for copy in d_out(l, 3):
                    copy.start()
            add_dx((n - 1) * few, 3, 1, few)

    last = []
    for q in (2, 3):
        round_dx(q, q - 2)
        for away in range(sources):
            block = gx.at[q, flip(ex, away)]
            last.append(pltpu.make_async_copy(block, out_dx[away].at[q - 2], far_sem.at[q - 2, away]))
            last[-1].start()
    for j in range(2):
        near.end(j)
    home_copy = pltpu.make_async_copy(near.home, out_home, own_send.at[0, 0])
    home_copy.start()

    @pl.loop(0, local)
    def _(l):
        for q in (2, 1):
            exchange(l, q).wait_send()
        for way in range(3):
            grads_to(l, way).wait_send()
        for q in range(replicas):
            for copy in d_out(l, q):
                copy.wait()

        @pl.when(l >= local - ring)
        def _():
            for copy in row_out(l, 0):
                copy.wait()

    for q in order:
        for n in range(3):
            if q:
                first(q, n).wait_send()
            if n != 1:
                sent_blocks(q, n)
    for copy in (*last, home_copy):
        copy.wait()


def forward(inputs, out_grad, meta, weights, replicas, sources, cap):
    tok = inputs.shape[0]
    part, local, kinds, ffn = weights.shape
    width = kinds * ffn
    chunk = part // 16
    ring = min(4, local)
    slots = sources * cap
    dims = (replicas, sources, tok, part, local, slots, ffn, cap)
    any_spec = pl.BlockSpec(memory_space=pl.ANY)
    rows = (replicas, local, slots)
    dma = pltpu.SemaphoreType.DMA
    return pl.pallas_call(
        functools.partial(forward_kernel, dims),
        out_shape=(
            jax.ShapeDtypeStruct((*rows, part), BF16),
            jax.ShapeDtypeStruct((*rows, part), BF16),
            jax.ShapeDtypeStruct((*rows, 2 * ffn), BF16),
            jax.ShapeDtypeStruct((*rows, ffn), BF16),
            *[jax.ShapeDtypeStruct((2, tok, part), BF16)] * (1 + sources),
        ),
        in_specs=[any_spec] * 4,
        out_specs=(any_spec,) * (5 + sources),
        scratch_shapes=[
            pltpu.VMEM((replicas, sources, tok, part), BF16),
            pltpu.VMEM((replicas, sources, tok, part), BF16),
            pltpu.VMEM((replicas, sources, *meta.shape), BF16),
            pltpu.VMEM((local, part, width), BF16),
            pltpu.VMEM((replicas, local, sources * tok), F32),
            pltpu.VMEM((local, sources * tok), F32),
            pltpu.VMEM((ring, slots, part), BF16),
            pltpu.VMEM((ring, slots, part), BF16),
            pltpu.VMEM((2, local, slots, width), BF16),
            pltpu.VMEM((3, local, slots, width), BF16),
            pltpu.VMEM((local, slots, width), F32),
            pltpu.VMEM((*rows, width), BF16),
            pltpu.VMEM((2, chunk, kinds, local, ffn), BF16),
            pltpu.VMEM((width // 128, local * chunk, 128), F32),
            pltpu.VMEM((2, sources * tok, part), F32),
            dma((replicas, 3)),
            dma((replicas, 3, sources)),
            dma((3, replicas, 3, sources)),
            dma((2,)),
            dma((replicas, local)),
            dma((3, local)),
            dma((3, local)),
            dma((3, local)),
            dma((2, replicas, local)),
            dma((2, ring)),
            dma((2, sources)),
            *scatter_scratch(2, sources, tok, part),
        ],
        compiler_params=pltpu.CompilerParams(
            collective_id=0, has_side_effects=True, vmem_limit_bytes=63 << 20
        ),
        name="gather_forward",
    )(inputs, out_grad, meta, weights.transpose(0, 2, 1, 3))


def by_collectives(inputs, out_grad, terms, weights, top, sources, swap):
    replicas = lax.axis_size("rep")
    me = lax.axis_index("rep")
    tok_dev = inputs.shape[0]
    part, local, kinds, ffn = weights.shape
    pair = 2 * ffn
    slots = sources * CAP
    half = max(replicas // 2, 1)
    mats = weights.transpose(1, 0, 2, 3).reshape(local, part, kinds * ffn)
    meta = jnp.concatenate(terms).reshape(-1, part)
    meta_rows = meta.shape[0]
    pad = -meta_rows % 16
    meta = jnp.pad(meta, ((0, pad), (0, 0)))

    def arrive(q):
        at = (me ^ q) * part
        x = lax.dynamic_slice_in_dim(inputs, at, part, 1)
        g = lax.dynamic_slice_in_dim(out_grad, at, part, 1)
        return swap(jnp.concatenate([x, g, meta]), q)

    gathered = {}
    for start in range(replicas - half, -1, -half):
        chosen = range(start, start + half)
        block = jnp.stack([arrive(q) for q in reversed(chosen)])
        block = lax.all_gather(block, "exp", axis=0, tiled=False)
        for place, q in enumerate(reversed(chosen)):
            gathered[q] = block[:, place]

    mine = lax.axis_index("exp") * local + jnp.arange(local, dtype=jnp.int32)
    earlier = jnp.arange(tok_dev)[:, None] < jnp.arange(tok_dev)[None, :]
    base = (jnp.arange(sources) * CAP).astype(F32)
    pair_mats, down_mats = mats[..., :pair], mats[..., pair:]
    picks, rows_x, rows_g, arrivals = {}, {}, {}, {}
    for q in reversed(range(replicas)):
        if q == half - 1 and replicas > 1:
            later = {p: gathered[p] for p in range(half)}
            later, _ = lax.optimization_barrier((later, sent))
            gathered.update(later)
        got = gathered[q]
        info = got[:, 2 * tok_dev : 2 * tok_dev + meta_rows].astype(F32)
        info = info.reshape(sources, 4, top, tok_dev)
        weight = info[:, 1] + info[:, 2] + info[:, 3]
        hit = info[:, 0][None] == mine.astype(F32)[:, None, None, None]
        named = jnp.any(hit, axis=2)
        gate = jnp.sum(jnp.where(hit, weight[None], 0.0), axis=2)
        rank = jnp.einsum(
            "let,tu->leu", named.astype(BF16), earlier.astype(BF16), preferred_element_type=F32
        )
        rank = jnp.where(named, rank + base[None, :, None], -1.0)
        rank = rank.reshape(local, 1, sources * tok_dev)
        onehot = rank == jnp.arange(slots, dtype=F32)[None, :, None]
        gate = gate.reshape(local, 1, sources * tok_dev)
        gate_slot = jnp.sum(jnp.where(onehot, gate, 0.0), axis=2)
        picks[q] = onehot.astype(BF16)
        tokens_x = got[:, :tok_dev].reshape(sources * tok_dev, part)
        tokens_g = got[:, tok_dev : 2 * tok_dev].reshape(sources * tok_dev, part)
        x = jnp.einsum("lst,td->lsd", picks[q], tokens_x, preferred_element_type=F32)
        g = jnp.einsum("lst,td->lsd", picks[q], tokens_g, preferred_element_type=F32)
        rows_x[q] = x.astype(BF16)
        rows_g[q] = (g * gate_slot[..., None]).astype(BF16)
        hidden = jnp.einsum("lrd,ldh->lrh", rows_x[q], pair_mats, preferred_element_type=F32)
        da = jnp.einsum("lrd,ldh->lrh", rows_g[q], down_mats, preferred_element_type=F32)
        sums = [hidden, da]
        for term in arrivals.pop(q, []):
            sums = [old + new.astype(F32) for old, new in zip(sums, term)]
        sent = [one.astype(BF16) for one in sums]
        if q:
            arrivals.setdefault(q & (q - 1), []).append([swap(one, q & -q) for one in sent])

    hidden, da = sums
    hg, hu = hidden[..., :ffn], hidden[..., ffn:]
    sig = jax.nn.sigmoid(hg)
    act = (hg * sig * hu).astype(BF16)
    dhu = (da * hg * sig).astype(BF16)
    dhg = (da * hu * sig * (1.0 + hg * (1.0 - sig))).astype(BF16)
    d_pair, acts = {0: jnp.concatenate([dhg, dhu], axis=2)}, {0: act}
    for held in (d_pair, acts):
        bit = replicas // 2
        while bit:
            for q in list(held):
                held[q ^ bit] = swap(held[q], bit)
            bit //= 2

    token_dx = {}
    for q in range(replicas):
        slot_dx = jnp.einsum(
            "lrh,ldh->lrd", d_pair[q], pair_mats, preferred_element_type=F32
        ).astype(BF16)
        dx = jnp.einsum("lst,lsd->td", picks[q], slot_dx, preferred_element_type=F32)
        token_dx[q] = dx.astype(BF16).reshape(sources, tok_dev, part)
    home = {}
    for start in range(0, replicas, half):
        block = jnp.concatenate([token_dx[q] for q in range(start, start + half)], axis=1)
        block = lax.psum_scatter(block, "exp", scatter_dimension=0, tiled=False)
        for place in range(half):
            one = block[place * tok_dev : (place + 1) * tok_dev]
            home[start + place] = swap(one, start + place)
    home = jnp.stack([home[q] for q in range(replicas)])

    def stacked(pieces):
        return jnp.stack([pieces[q] for q in range(replicas)])

    return stacked(rows_x), stacked(rows_g), stacked(d_pair), stacked(acts), home


def per_device(inputs, out_grad, routes, gates, weights, moment_one, moment_two):
    replicas, sources = lax.axis_size("rep"), lax.axis_size("exp")
    tok_dev, top = routes.shape
    part, local, kinds, ffn = weights.shape
    slots = sources * CAP
    me = lax.axis_index("rep")

    def swap(array, bits):
        if bits == 0:
            return array
        return lax.ppermute(array, "rep", [(i, i ^ bits) for i in range(replicas)])

    terms, rest = [routes.astype(BF16).T], gates.T
    for _ in range(3):
        head = lax.reduce_precision(rest, 8, 7)
        terms.append(head.astype(BF16))
        rest = rest - head
    at_once = 2 * replicas * sources * tok_dev * part + 20 * local * slots * kinds * ffn
    if replicas == 4 and sources >= 2 and sources & (sources - 1) == 0 and at_once < 32 << 20:
        meta = jnp.concatenate(terms, axis=1)
        meta = jnp.pad(meta, ((0, -top % 16), (0, 0)))
        *grown, near, own_dx = (outs := forward(
            inputs, out_grad, meta, weights, replicas, sources, CAP
        ))[:6]
        came = []
        for away, block in enumerate(outs[6:], 1):
            pairs = [(i, i ^ away) for i in range(sources)]
            came.append(lax.ppermute(block, "exp", pairs))
        first_moment, second_moment, new_weights = expert_update(
            *grown, weights, moment_one, moment_two
        )
        far = sum([block.astype(F32) for block in came], own_dx.astype(F32)).astype(BF16)
        far = [swap(far[j], j + 2) for j in range(2)]
        home = jnp.concatenate([near, jnp.stack(far)])
    else:
        *grown, home = by_collectives(inputs, out_grad, terms, weights, top, sources, swap)
        first_moment, second_moment, new_weights = expert_update(
            *grown, weights, moment_one, moment_two
        )
    input_grad = jnp.concatenate(
        [lax.dynamic_index_in_dim(home, me ^ q, 0, keepdims=False) for q in range(replicas)],
        axis=1,
    )
    return (input_grad, first_moment, second_moment, new_weights)


def solution(mesh):
    tokens = P(("rep", "exp"), None)
    experts = P("rep", "exp", None, None)
    return jax.shard_map(
        per_device,
        mesh=mesh,
        in_specs=(tokens, tokens, tokens, tokens, experts, experts, experts),
        out_specs=(tokens, experts, experts, experts),
        check_vma=False,
    )
```
